128 devices in a mesh: dense: 32 (over x, z, core), attn: 4 (over y).
Axes of the slice: x: 4, y: 4, z: 4, core: 2. Of those that a mesh axis runs over, the one named last changes fastest.
Arguments:
- queries: bfloat16 [8192, 4096], P('dense', 'attn'), may hold values from -30 to 30
- keys: bfloat16 [8192, 1024], P('dense', 'attn'), may hold values from -13 to 13
- values: bfloat16 [8192, 1024], P('dense', 'attn'), may hold values from -24 to 24
- segments: int32 [8192], replicated, may hold values from 0 to 5, never falling along the last dimension, each value on 1 to 4096 neighbouring positions
- out_weight: bfloat16 [4096, 4096], P('attn', 'dense'), may hold values from -0.09375 to 0.09375
Outputs:
- projected: bfloat16 [8192, 4096], P('dense', 'attn')
The draws below stay inside these ranges and needn't reach their ends.
All inputs are finite; a program needn't handle non-finite values.
Results may differ from the reference program's by a relative error of at most 0.012.
Values may be sent and summed in bfloat16 or wider, within the bound.
A program may use at most 128 MiB of HBM per device.

```python
import math
import jax
import jax.numpy as jnp
import numpy as np
from jax import lax

D = 4096
QUERY_HEAD_COUNT = 32
KEY_VALUE_HEADS = 8
HEAD_WIDTH = 128
DOCS = 6
WINDOW_TOKENS = 8192


def draw_queries(key, part):
    base_offset = jax.random.normal(jax.random.fold_in(key, 601), (WINDOW_TOKENS, QUERY_HEAD_COUNT * HEAD_WIDTH), jnp.float32)
    queries = 1.5 * jnp.clip(base_offset, -5.0, 5.0)
    return queries.astype(jnp.bfloat16)


def draw_keys(key, part):
    base_offset = jax.random.normal(jax.random.fold_in(key, 701), (WINDOW_TOKENS, KEY_VALUE_HEADS * HEAD_WIDTH), jnp.float32)
    keys = jnp.clip(base_offset, -5.0, 5.0)
    return keys.astype(jnp.bfloat16)


def level_of(key, extent, cuts, low, high):
    def one(dim, shards_of):
        steps = jax.random.uniform(jax.random.fold_in(jax.random.fold_in(key, 6), dim), (shards_of,), jnp.float32, low / len(cuts), high / len(cuts))
        return jnp.repeat(jnp.exp(steps), extent[dim] // shards_of).reshape((-1,) + (1,) * (len(extent) - dim - 1))

    level = one(*cuts[0])
    for cut in cuts[1:]:
        level = level * one(*cut)
    return level


def profile(number_of, total, most, lean):
    portions = [(1 << 20) // math.isqrt(rank ** lean) + 1 for rank in range(2, number_of + 1)]
    rest, counts = total - most - (number_of - 1), [1] * (number_of - 1)
    while rest > 0:
        movable = [i for i in range(number_of - 1) if counts[i] < most]
        mass, budget = sum([portions[i] for i in movable]), rest
        for i in movable:
            addition = min(most - counts[i], max(1, budget * portions[i] // mass), rest)
            counts[i] = counts[i] + addition
            rest = rest - addition
    return np.array([most] + counts)


def ragged(rng, amount, total, bound, lean):
    if amount == 2:
        one = jax.random.randint(rng, (), max(1, total - bound), min(bound, total - 1) + 1)
        return jnp.stack([one, total - one])
    sizes = jnp.asarray(profile(amount, total, bound, lean), jnp.int32)
    pairs = (amount - 1) // 2
    source_of, sink = sizes[1:1 + 2 * pairs:2], sizes[2:2 + 2 * pairs:2]
    slack = jnp.minimum(source_of - 1, bound - sink)
    passed = jax.random.randint(jax.random.fold_in(rng, 1), (pairs,), 0, 1 << 20) % (slack + 1)
    sizes = sizes.at[1:1 + 2 * pairs:2].set(source_of - passed).at[2:2 + 2 * pairs:2].set(sink + passed)
    return sizes[jax.random.permutation(jax.random.fold_in(rng, 2), amount)]


def noise(rng, shape, deviation, most, split=(), kind=jnp.bfloat16):
    factor_of = level_of(rng, shape, split, -0.22, 0.18) if split else 1.0
    result = jax.random.normal(rng, shape, jnp.float32) * deviation * factor_of
    return jnp.minimum(jnp.maximum(result, -most), most).astype(kind)


def setup_inputs(seed: int = 0) -> dict:
    key_list = jax.random.split(jax.random.key(seed), 6)
    queries = draw_queries(jax.random.fold_in(key_list[5], 71), 0)
    keys = draw_keys(jax.random.fold_in(key_list[5], 71), 0)
    values = noise(key_list[2], (WINDOW_TOKENS, KEY_VALUE_HEADS * HEAD_WIDTH), 4.0, 24.0, ((0, 32), (1, 4)))
    segments = jnp.searchsorted(jnp.cumsum(ragged(key_list[3], DOCS, WINDOW_TOKENS, WINDOW_TOKENS // 2, 2)), jnp.arange(WINDOW_TOKENS), side="right").astype(jnp.int32)
    out_weight = noise(key_list[4], (QUERY_HEAD_COUNT * HEAD_WIDTH, D), (QUERY_HEAD_COUNT * HEAD_WIDTH) ** -0.5, 0.09375, ((0, 4), (1, 32)))
    return {"queries": queries, "keys": keys, "values": values, "segments": segments, "out_weight": out_weight}


NEGATIVE = -1e+30

def reference(queries, keys, values, segments, out_weight):
    head_group = QUERY_HEAD_COUNT // KEY_VALUE_HEADS
    inv_root = 1.0 / math.sqrt(HEAD_WIDTH)
    rows_block = min(1024, WINDOW_TOKENS)
    blocks_count = WINDOW_TOKENS // rows_block
    positions = jnp.arange(WINDOW_TOKENS, dtype=jnp.int32)
    query_split = queries.reshape(blocks_count, rows_block, QUERY_HEAD_COUNT, HEAD_WIDTH)

    def one_task(task):
        head = task // blocks_count
        which = task % blocks_count
        sliced = lax.dynamic_index_in_dim(query_split, which, 0, keepdims=False)
        query_head = lax.dynamic_index_in_dim(sliced, head, 1, keepdims=False)
        column = (head // head_group * HEAD_WIDTH).astype(jnp.int32)
        key_head = lax.dynamic_slice_in_dim(keys, column, HEAD_WIDTH, 1)
        value_head = lax.dynamic_slice_in_dim(values, column, HEAD_WIDTH, 1)
        lower = (which * rows_block).astype(jnp.int32)
        query_pos = lower + jnp.arange(rows_block, dtype=jnp.int32)
        query_docs = lax.dynamic_slice_in_dim(segments, lower, rows_block)
        visible = (query_docs[:, None] == segments[None, :]) & (positions[None, :] <= query_pos[:, None])
        scores = jnp.dot(query_head, key_head.T, preferred_element_type=jnp.float32) * inv_root
        scores = jnp.where(visible, scores, NEGATIVE)
        row_max = lax.optimization_barrier(jnp.max(scores, axis=-1))
        expd = jnp.where(visible, jnp.exp(scores - row_max[:, None]), 0.0)
        totals = lax.optimization_barrier(jnp.sum(expd, axis=-1))
        mixed = jnp.dot(expd.astype(jnp.bfloat16), value_head, preferred_element_type=jnp.float32) / totals[:, None]
        return mixed.astype(jnp.bfloat16)
    results = lax.map(one_task, jnp.arange(QUERY_HEAD_COUNT * blocks_count, dtype=jnp.int32))
    attended = results.reshape(QUERY_HEAD_COUNT, blocks_count, rows_block, HEAD_WIDTH).transpose(1, 2, 0, 3).reshape(WINDOW_TOKENS, QUERY_HEAD_COUNT * HEAD_WIDTH)
    return jnp.dot(attended, out_weight, preferred_element_type=jnp.float32).astype(jnp.bfloat16)
```

```python
import math

import jax
import jax.numpy as jnp
from jax import lax
from jax.experimental import pallas as pl
from jax.experimental.pallas import tpu as pltpu
from jax.sharding import PartitionSpec as P

MESH = pl.DeviceIdType.MESH
BF = jnp.bfloat16
F32 = jnp.float32
HW = 128
TOK = 512
BIG = 32768.0
SCALE = math.log2(math.e) / math.sqrt(HW)
RT = 256
WA = 320


def kernel(q_hbm, k_hbm, v_hbm, seg_ref, w_hbm, out_hbm,
           qbuf, kvbuf, kabuf, wbuf, m_ref, acc_ref, abuf, psend, precv, pown, fin,
           local_sem, pair_send, pair_recv, kv_recv, w_recv, send_sem, p_send, p_recv, fin_local, fin_send, fin_recv):
    d = lax.axis_index("dense")
    y = lax.axis_index("attn")
    core = lax.rem(d, 2)
    chip = d // 2
    z = lax.rem(chip, 4)
    x = chip // 4
    true = None

    def mod4(n):
        return lax.rem(n + 8, 4)

    def chip_at(dx, dz):
        return mod4(x + dx) * 4 + mod4(z + dz)

    def device_at(dx, dz):
        return (chip_at(dx, dz) * 2 + core, y)

    partner = (chip * 2 + (1 - core), y)

    def when(pred, f):
        if pred is None:
            f()
        else:
            pl.when(pred)(f)

    sends = []

    def both(p, r):
        if p is None:
            return r
        if r is None:
            return p
        return jnp.logical_and(p, r)

    def send(ref_of, recv_sems, dx, dz, ddx, ddz, pred=None, src=None):
        n = len(sends)
        slot = ref_of(chip_at(dx, dz))
        rel = ((dx - ddx) % 4) * 4 + (dz - ddz) % 4

        def make():
            return pltpu.make_async_remote_copy(
                src_ref=slot if src is None else src, dst_ref=slot,
                send_sem=send_sem.at[n], recv_sem=recv_sems(rel),
                device_id=device_at(ddx, ddz), device_id_type=MESH)

        sends.append((pred, make))
        when(pred, lambda: make().start())

    def wait(ref_of, recv_sems, dx, dz, pred=None):
        rel = (dx % 4) * 4 + dz % 4
        slot = ref_of(chip_at(dx, dz))
        when(pred, lambda: pltpu.make_async_remote_copy(
            src_ref=slot, dst_ref=slot, send_sem=send_sem.at[0], recv_sem=recv_sems(rel),
            device_id=partner, device_id_type=MESH).wait_recv())

    def kv_of(j):
        return lambda c: kvbuf.at[c, j]

    def kv_sems(j):
        return lambda rel: kv_recv.at[j, rel]

    def kv_send(j, dx, dz, ddx, ddz, pred=None):
        send(kv_of(j), kv_sems(j), dx, dz, ddx, ddz, pred)

    def kv_wait(j, dx, dz, pred=None):
        wait(kv_of(j), kv_sems(j), dx, dz, pred)

    def w_part(t):
        return (0, WA) if t == 0 else (WA, 1024 - WA)

    def w_of(t):
        lo, n = w_part(t)
        return lambda c: wbuf.at[c, pl.ds(lo, n)]

    def w_sems(t):
        return lambda rel: w_recv.at[t, rel]

    def w_send(t, dx, dz, ddx, ddz, src=None):
        send(w_of(t), w_sems(t), dx, dz, ddx, ddz, None, src)

    def w_wait(t, dx, dz):
        wait(w_of(t), w_sems(t), dx, dz)

    def own_cols(ref, width, which):
        return ref.at[:, pl.ds(pl.multiple_of(which * width, width), width)]

    rows_me = pl.ds(pl.multiple_of(core * 256, 256), 256)
    locals_ = [
        pltpu.make_async_copy(own_cols(k_hbm, HW, core), kvbuf.at[chip, 0, rows_me], local_sem.at[0]),
        pltpu.make_async_copy(own_cols(v_hbm, HW, core), kvbuf.at[chip, 1, rows_me], local_sem.at[1]),
        pltpu.make_async_copy(own_cols(q_hbm, 512, core), qbuf.at[rows_me], local_sem.at[2]),
        pltpu.make_async_copy(w_hbm, wbuf.at[chip], local_sem.at[3]),
    ]
    for c in locals_:
        c.start()

    barrier = pltpu.get_barrier_semaphore()
    peers = [partner, device_at(1, 0), device_at(-1, 0), device_at(0, 1), device_at(0, -1)]
    peers += [(d, mod4(y + n)) for n in (1, 2, 3)]
    for peer in peers:
        pl.semaphore_signal(barrier, inc=1, device_id=peer, device_id_type=MESH)
    pl.semaphore_wait(barrier, len(peers))

    pair = []
    for n, (src, dst) in enumerate((
            (own_cols(k_hbm, HW, 1 - core), kvbuf.at[chip, 0, rows_me]),
            (own_cols(v_hbm, HW, 1 - core), kvbuf.at[chip, 1, rows_me]),
            (own_cols(q_hbm, 512, 1 - core), qbuf.at[rows_me]))):
        pair.append(pltpu.make_async_remote_copy(
            src_ref=src, dst_ref=dst, send_sem=pair_send.at[n], recv_sem=pair_recv.at[n],
            device_id=partner, device_id_type=MESH))
        pair[-1].start()

    for j in (0, 1):
        locals_[j].wait()
        pair[j].wait_recv()
        kv_send(j, 0, 0, 1, 0, x <= 2)
        kv_send(j, 0, 0, 0, 1, z <= 2)
        kv_send(j, 0, 0, 0, -1, z == 0)

    def w_own(t):
        lo, n = w_part(t)
        return w_hbm.at[pl.ds(lo, n)]

    for ddx, ddz in ((0, 1), (0, -1), (-1, 0), (1, 0)):
        for t in (1, 0):
            w_send(t, 0, 0, ddx, ddz, w_own(t))

    def onehot(c):
        row = seg_ref[pl.ds(c, 1), :]
        hot = (lax.broadcasted_iota(jnp.int32, (HW, TOK), 0) == row).astype(F32)
        return hot.T

    own_hot = onehot(chip)
    qa = (own_hot * (-BIG)).astype(BF)

    r1 = x >= 1
    r2 = x >= 2

    def scores(h, half, keys):
        qq = qbuf[half * RT:(half + 1) * RT, h * HW:(h + 1) * HW]
        qc = jnp.concatenate([qq, qa[half * RT:(half + 1) * RT]], axis=1)
        return lax.dot_general(qc, keys, (((1,), (1,)), ((), ())), preferred_element_type=F32)

    def weights(s, mp):
        mc = jnp.max(s, axis=1, keepdims=True)
        mn = jnp.maximum(mp, mc) if mp is not None else jnp.broadcast_to(mc, (RT, HW))
        p = jnp.exp2(s * SCALE - (mn * SCALE)[:, :1])
        return mn, p.astype(BF)

    tiles = [(h, half) for h in range(4) for half in range(2)]

    def own_block():
        keys = jnp.concatenate([kvbuf[chip, 0], (1.0 - own_hot).astype(BF)], axis=1)
        vals = jnp.concatenate([kvbuf[chip, 1], jnp.ones((TOK, HW), BF)], axis=1)

        def masked(h, half):
            n = (half + 1) * RT
            s = scores(h, half, keys[:n])
            r = lax.broadcasted_iota(jnp.int32, (RT, n), 0) + half * RT
            c = lax.broadcasted_iota(jnp.int32, (RT, n), 1)
            return jnp.where(c <= r, s, -2.0 * BIG)

        s = masked(*tiles[0])
        for i, (h, half) in enumerate(tiles):
            nxt = masked(*tiles[i + 1]) if i < 7 else None
            mn, p = weights(s, None)
            rows = slice((h * 2 + half) * RT, (h * 2 + half + 1) * RT)
            m_ref[rows] = mn
            acc_ref[rows] = jnp.dot(p, vals[:(half + 1) * RT], preferred_element_type=F32)
            s = nxt

    def put_mask(c, valid, n):
        hot = onehot(c)
        kabuf[n * TOK:(n + 1) * TOK] = jnp.where(valid, 1.0 - hot, 1.0).astype(BF)

    def two_blocks(ca, cb, part):
        keys = jnp.concatenate([
            jnp.concatenate([kvbuf[ca, 0], kvbuf[cb, 0]], axis=0), kabuf[...]], axis=1)
        vals = jnp.concatenate([
            jnp.concatenate([kvbuf[ca, 1], kvbuf[cb, 1]], axis=0), jnp.ones((2 * TOK, HW), BF)], axis=1)
        todo = tiles[part * 4:part * 4 + 4]
        s = scores(*todo[0], keys)
        for i, (h, half) in enumerate(todo):
            rows = slice((h * 2 + half) * RT, (h * 2 + half + 1) * RT)
            mp = m_ref[rows]
            old = acc_ref[rows]
            nxt = scores(*todo[i + 1], keys) if i < 3 else None
            mn, p = weights(s, mp)
            al = jnp.exp2((mp - mn) * SCALE)
            add = jnp.dot(p, vals, preferred_element_type=F32)
            m_ref[rows] = mn
            acc_ref[rows] = old * jnp.concatenate([al, al], axis=1) + add
            s = nxt

    def kv_x1():
        for j in (0, 1):
            kv_wait(j, -1, 0, r1)
            kv_send(j, -1, 0, 1, 0, both(r1, x <= 2))
            kv_send(j, -1, 0, 0, 1, r1)
            kv_send(j, -1, 0, 0, -1, r1)

    def kv_row0():
        for j in (0, 1):
            kv_wait(j, 0, -1, z >= 1)
            kv_send(j, 0, -1, 0, 1, jnp.logical_or(z == 1, z == 2))

    def kv_x2():
        for j in (0, 1):
            kv_wait(j, -2, 0, r2)
            kv_send(j, -2, 0, 0, -1, both(r2, z >= 1))
            kv_send(j, -2, 0, 0, 1, both(r2, z == 3))

    edge = jnp.logical_or(z == 0, z == 3)
    middle = jnp.logical_or(z == 1, z == 2)

    def kv_row1():
        for j in (0, 1):
            kv_wait(j, -1, -1, r1)
            kv_send(j, -1, -1, 0, 1, both(r1, edge))
            kv_wait(j, -1, 1, r1)
            kv_send(j, -1, 1, 0, -1, both(r1, edge))

    def kv_row2():
        for j in (0, 1):
            kv_wait(j, -2, 1, both(r2, z <= 2))
            kv_send(j, -2, 1, 0, -1, both(r2, middle))

    def kv_last():
        for j in (0, 1):
            kv_wait(j, 0, -2, z >= 2)
            kv_wait(j, 0, 1, z == 3)
            kv_wait(j, -1, 2, r1)
            kv_wait(j, -2, -1, both(r2, z == 0))

    def kv_end():
        for j in (0, 1):
            kv_wait(j, -2, 2, both(r2, z <= 1))

    def place(t, a, b):
        return (a, b) if t == 0 else (b, a)

    def w_first(t, a):
        w_wait(t, *place(t, a, 0))
        if t == 0 and a == -1 or t == 1 and a == 1:
            w_send(t, *place(t, a, 0), *place(t, -a, 0))
        for s in (1, -1):
            w_send(t, *place(t, a, 0), *place(t, 0, s))

    def w_second(t, a, b, relay):
        w_wait(t, *place(t, a, b))
        if relay:
            w_send(t, *place(t, a, b), *place(t, 0, -b))

    def relay2(t, a):
        if t == 1:
            return 1
        return 1 if a in (0, 2) else -1

    def w_far(t):
        w_wait(t, *place(t, 2, 0))
        for s in (1, -1):
            w_send(t, *place(t, 2, 0), *place(t, 0, s))

    def w_line(t, a):
        r = relay2(t, a)
        w_second(t, a, r, True)
        w_second(t, a, -r, False)

    def w_line_far(t, a):
        w_wait(t, *place(t, a, 2))

    locals_[2].wait()
    pair[2].wait_recv()
    own_block()
    kv_x1()
    kv_row0()
    kv_x2()

    def pick(dz):
        zs = mod4(z + dz)
        before = zs < z
        c = jnp.where(before, x * 4, mod4(x - 2) * 4) + zs
        return c, jnp.logical_or(before, r2)

    steps = [
        ((chip_at(-1, 0), r1), (chip_at(-2, 0), r2)),
        ((chip_at(-1, -1), r1), (chip_at(-1, 1), r1)),
        ((chip_at(-1, 2), r1), pick(-1)),
        (pick(1), pick(2)),
    ]
    before = [[], [kv_row1], [kv_row2, kv_last], [kv_end]]
    between = [
        [[lambda: w_first(1, 1), lambda: w_first(1, -1)], [lambda: w_first(0, -1), lambda: w_first(0, 1)]],
        [[lambda: w_line(1, 0)], [lambda: w_far(1)]],
        [[lambda: w_far(0)], [lambda: w_line(0, 0)]],
        [[lambda: w_line(1, 1)], [lambda: w_line(1, -1)]],
    ]

    for s in range(4):
        (ca, va), (cb, vb) = steps[s]
        for f in before[s]:
            f()
        live = jnp.logical_or(va, vb)
        ca = jnp.where(va, ca, chip)
        cb = jnp.where(vb, cb, chip)

        def masks():
            put_mask(ca, va, 0)
            put_mask(cb, vb, 1)

        pl.when(live)(masks)
        for part in (0, 1):
            pl.when(live)(lambda: two_blocks(ca, cb, part))
            for f in between[s][part]:
                f()

    for h in range(4):
        rows = slice(h * TOK, (h + 1) * TOK)
        abuf[core, :, h * HW:(h + 1) * HW] = (acc_ref[rows, :HW] / acc_ref[rows, HW:]).astype(BF)
    swap = pltpu.make_async_remote_copy(
        src_ref=abuf.at[core], dst_ref=abuf.at[core], send_sem=pair_send.at[3], recv_sem=pair_recv.at[3],
        device_id=partner, device_id_type=MESH)
    swap.start()

    for a in (1, -1):
        w_line(0, a)
    w_line(1, 2)
    w_line(0, 2)
    locals_[3].wait()
    swap.wait_recv()

    def quarter(qr, pairs):
        lhs = [abuf[0], abuf[1]]
        for n in pairs:
            wcat = jnp.concatenate([wbuf[qr * 4 + 2 * n], wbuf[qr * 4 + 2 * n + 1]], axis=1)
            part = jnp.dot(lhs[0], wcat[:512], preferred_element_type=F32)
            part += jnp.dot(lhs[1], wcat[512:], preferred_element_type=F32)
            mine = qr == y

            def keep():
                pown[n] = part

            def give():
                slot = mod4(qr - y) - 1
                psend[slot, n] = part.astype(BF)
                p_copy(slot, n).start()

            pl.when(mine)(keep)
            pl.when(jnp.logical_not(mine))(give)

    def p_copy(slot, n):
        return pltpu.make_async_remote_copy(
            src_ref=psend.at[slot, n], dst_ref=precv.at[slot, n],
            send_sem=p_send.at[slot, n], recv_sem=p_recv.at[slot, n],
            device_id=(d, mod4(y + slot + 1)), device_id_type=MESH)

    for a in (0, 1, -1, 2):
        w_line_far(0, a)
    for b in (0, 1, -1, 2):
        w_line_far(1, b)
    for dq in (0, 1, -1, 2):
        quarter(mod4(x + dq), (0, 1))

    for n in (0, 1):
        for slot in range(3):
            p_copy(slot, n).wait_recv()
        total = pown[n]
        for slot in range(3):
            total += precv[slot, n].astype(F32)
        fin[n] = total.astype(BF)
    ends = []
    rows_you = pl.ds(pl.multiple_of((1 - core) * 256, 256), 256)
    for n in range(4):
        cols = pl.ds(pl.multiple_of((2 * n + core) * HW, HW), HW)
        lanes = pl.ds((n % 2) * HW, HW)
        far = pltpu.make_async_remote_copy(
            src_ref=fin.at[n // 2, rows_you, lanes], dst_ref=out_hbm.at[:, cols],
            send_sem=fin_send.at[n], recv_sem=fin_recv.at[n], device_id=partner, device_id_type=MESH)
        far.start()
        near = pltpu.make_async_copy(fin.at[n // 2, rows_me, lanes], out_hbm.at[:, cols], fin_local.at[n])
        near.start()
        ends.append((far, near))
    for far, near in ends:
        far.wait()
        near.wait()
    for c in pair:
        c.wait_send()
    swap.wait_send()
    for pred, make in sends:
        when(pred, lambda: make().wait_send())
    for slot in range(3):
        for n in (0, 1):
            p_copy(slot, n).wait_send()


def shards(queries, keys, values, segments, out_weight):
    return pl.pallas_call(
        kernel,
        out_shape=jax.ShapeDtypeStruct((256, 1024), BF),
        in_specs=[
            pl.BlockSpec(memory_space=pl.ANY),
            pl.BlockSpec(memory_space=pl.ANY),
            pl.BlockSpec(memory_space=pl.ANY),
            pl.BlockSpec(memory_space=pltpu.VMEM),
            pl.BlockSpec(memory_space=pl.ANY),
        ],
        out_specs=pl.BlockSpec(memory_space=pl.ANY),
        scratch_shapes=[
            pltpu.VMEM((TOK, 512), BF),
            pltpu.VMEM((16, 2, TOK, HW), BF),
            pltpu.VMEM((2 * TOK, HW), BF),
            pltpu.VMEM((16, 1024, HW), BF),
            pltpu.VMEM((2048, HW), F32),
            pltpu.VMEM((2048, 2 * HW), F32),
            pltpu.VMEM((2, TOK, 512), BF),
            pltpu.VMEM((3, 2, TOK, 256), BF),
            pltpu.VMEM((3, 2, TOK, 256), BF),
            pltpu.VMEM((2, TOK, 256), F32),
            pltpu.VMEM((2, TOK, 256), BF),
            pltpu.SemaphoreType.DMA((4,)),
            pltpu.SemaphoreType.DMA((4,)),
            pltpu.SemaphoreType.DMA((4,)),
            pltpu.SemaphoreType.DMA((2, 16)),
            pltpu.SemaphoreType.DMA((2, 16)),
            pltpu.SemaphoreType.DMA((80,)),
            pltpu.SemaphoreType.DMA((3, 2)),
            pltpu.SemaphoreType.DMA((3, 2)),
            pltpu.SemaphoreType.DMA((4,)),
            pltpu.SemaphoreType.DMA((4,)),
            pltpu.SemaphoreType.DMA((4,)),
        ],
        compiler_params=pltpu.CompilerParams(
            collective_id=0, has_side_effects=True, vmem_limit_bytes=60 * 2**20),
        name="attention_projection",
    )(queries, keys, values, segments.reshape(16, TOK), out_weight)


def solution(mesh):
    return jax.shard_map(
        shards,
        mesh=mesh,
        in_specs=(
            P("dense", "attn"),
            P("dense", "attn"),
            P("dense", "attn"),
            P(),
            P("attn", "dense"),
        ),
        out_specs=P("dense", "attn"),
        check_vma=False,
    )
```

```python
import math

import jax
import jax.numpy as jnp
from jax import lax
from jax.experimental import pallas as pl
from jax.experimental.pallas import tpu as pltpu
from jax.sharding import PartitionSpec as P

MESH = pl.DeviceIdType.MESH
BF = jnp.bfloat16
F32 = jnp.float32
HW = 128
TOK = 512
BIG = 32768.0
SCALE = math.log2(math.e) / math.sqrt(HW)
RT = 256


def kernel(q_hbm, k_hbm, v_hbm, seg_ref, w_hbm, out_hbm,
           qbuf, kvbuf, kabuf, wbuf, m_ref, acc_ref, abuf, hold, own, far_out, far_in, near_out, near_in, fin,
           local_sem, pair_send, pair_recv, kv_recv, w_recv, send_sem, a_recv, far_recv, near_recv,
           fin_local, fin_recv):
    d = lax.axis_index("dense")
    y = lax.axis_index("attn")
    core = lax.rem(d, 2)
    chip = d // 2
    z = lax.rem(chip, 4)
    x = chip // 4

    def mod4(n):
        return lax.rem(n + 8, 4)

    def chip_at(dx, dz):
        return mod4(x + dx) * 4 + mod4(z + dz)

    def device_at(dx, dz):
        return (chip_at(dx, dz) * 2 + core, y)

    partner = (chip * 2 + (1 - core), y)
    pair_chip = x * 4 + (z + 1 - 2 * lax.rem(z, 2))
    cross = ((x * 4 + 3 - z) * 2 + core, y)

    def y_at(n):
        return (d, mod4(y + n))

    def when(pred, f):
        if pred is None:
            f()
        else:
            pl.when(pred)(f)

    def both(p, r):
        if p is None:
            return r
        if r is None:
            return p
        return jnp.logical_and(p, r)

    sends = []

    def send(src, dst, recv_sem, device, pred=None):
        n = len(sends)

        def make():
            return pltpu.make_async_remote_copy(
                src_ref=src, dst_ref=dst, send_sem=send_sem.at[n], recv_sem=recv_sem,
                device_id=device, device_id_type=MESH)

        sends.append((pred, make))
        when(pred, lambda: make().start())

    def wait(dst, recv_sem, pred=None):
        when(pred, lambda: pltpu.make_async_remote_copy(
            src_ref=dst, dst_ref=dst, send_sem=send_sem.at[0], recv_sem=recv_sem,
            device_id=partner, device_id_type=MESH).wait_recv())

    def kv_at(c, j, h):
        return kvbuf.at[c, j, pl.ds(pl.multiple_of(h * 256, 256), 256)]

    def kv_send(j, h, dx, dz, ddx, ddz, pred=None):
        slot = kv_at(chip_at(dx, dz), j, h)
        rel = ((dx - ddx) % 4) * 4 + (dz - ddz) % 4
        send(slot, slot, kv_recv.at[j * 2 + h, rel], device_at(ddx, ddz), pred)

    def kv_wait(j, h, dx, dz, pred=None):
        rel = (dx % 4) * 4 + dz % 4
        wait(kv_at(chip_at(dx, dz), j, h), kv_recv.at[j * 2 + h, rel], pred)

    pieces = [(j, h) for j in (0, 1) for h in (0, 1)]

    def w_at(s, row, piece):
        return wbuf.at[s, row, pl.ds(piece * 512, 512)]

    def w_send(s, piece, dx, ddx, src=None):
        slot = w_at(s, mod4(x + dx), piece)
        send(slot if src is None else src, slot, w_recv.at[s * 2 + piece, (dx - ddx) % 4], device_at(ddx, 0))

    def w_wait(s, piece, dx):
        wait(w_at(s, mod4(x + dx), piece), w_recv.at[s * 2 + piece, dx % 4])

    def cols_of(ref, width, which):
        return ref.at[:, pl.ds(pl.multiple_of(which * width, width), width)]

    rows_me = pl.ds(pl.multiple_of(core * 256, 256), 256)
    locals_ = [
        pltpu.make_async_copy(cols_of(k_hbm, HW, core), kv_at(chip, 0, core), local_sem.at[0]),
        pltpu.make_async_copy(cols_of(v_hbm, HW, core), kv_at(chip, 1, core), local_sem.at[1]),
        pltpu.make_async_copy(cols_of(q_hbm, 512, core), qbuf.at[rows_me], local_sem.at[2]),
        pltpu.make_async_copy(w_hbm, wbuf.at[0, x], local_sem.at[3]),
    ]
    for c in locals_:
        c.start()

    barrier = pltpu.get_barrier_semaphore()
    peers = [partner, device_at(1, 0), device_at(-1, 0), device_at(0, 1), device_at(0, -1),
             (pair_chip * 2 + (1 - core), y), y_at(1), y_at(-1)]
    for peer in peers:
        pl.semaphore_signal(barrier, inc=1, device_id=peer, device_id_type=MESH)
    pl.semaphore_wait(barrier, len(peers))

    pair = []
    for n, (src, dst) in enumerate((
            (cols_of(k_hbm, HW, 1 - core), kv_at(chip, 0, core)),
            (cols_of(v_hbm, HW, 1 - core), kv_at(chip, 1, core)),
            (cols_of(q_hbm, 512, 1 - core), qbuf.at[rows_me]))):
        pair.append(pltpu.make_async_remote_copy(
            src_ref=src, dst_ref=dst, send_sem=pair_send.at[n], recv_sem=pair_recv.at[n],
            device_id=partner, device_id_type=MESH))
        pair[-1].start()

    r1 = x >= 1
    r2 = x >= 2
    edge = jnp.logical_or(z == 0, z == 3)
    middle = jnp.logical_or(z == 1, z == 2)

    for mine in (True, False):
        for j in (0, 1):
            h = core if mine else 1 - core
            if mine:
                locals_[j].wait()
            else:
                pair[j].wait_recv()
            kv_send(j, h, 0, 0, 1, 0, x <= 2)
            kv_send(j, h, 0, 0, -1, 0, both(x <= 1, h == 1))
            kv_send(j, h, 0, 0, 0, 1, z <= 2)
            kv_send(j, h, 0, 0, 0, -1, z == 0)

    def w_cross(piece):
        send(w_hbm.at[pl.ds(piece * 512, 512)], w_at(1, x, piece), w_recv.at[2 + piece, 0], cross)

    w_cross(0)

    def onehot(c):
        row = jnp.concatenate([seg_ref[pl.ds(c * 4 + i, 1), :] for i in range(4)], axis=1)
        hot = (lax.broadcasted_iota(jnp.int32, (HW, TOK), 0) == row).astype(F32)
        return hot.T

    own_hot = onehot(chip)
    qa = (own_hot * (-BIG)).astype(BF)

    def scores(h, half, keys):
        qq = qbuf[half * RT:(half + 1) * RT, h * HW:(h + 1) * HW]
        qc = jnp.concatenate([qq, qa[half * RT:(half + 1) * RT]], axis=1)
        return lax.dot_general(qc, keys, (((1,), (1,)), ((), ())), preferred_element_type=F32)

    def weights(s, mp):
        mc = jnp.max(s, axis=1, keepdims=True)
        mn = jnp.maximum(mp, mc) if mp is not None else jnp.broadcast_to(mc, (RT, HW))
        p = jnp.exp2(s * SCALE - (mn * SCALE)[:, :1])
        return mn, p.astype(BF)

    tiles = [(h, half) for half in range(2) for h in range(4)]

    def tile_rows(h, half):
        return slice((h * 2 + half) * RT, (h * 2 + half + 1) * RT)

    def own_block():
        keys = jnp.concatenate([kvbuf[chip, 0], (1.0 - own_hot).astype(BF)], axis=1)
        vals = jnp.concatenate([kvbuf[chip, 1], jnp.ones((TOK, HW), BF)], axis=1)

        def masked(h, half):
            n = (half + 1) * RT
            s = scores(h, half, keys[:n])
            r = lax.broadcasted_iota(jnp.int32, (RT, n), 0) + half * RT
            c = lax.broadcasted_iota(jnp.int32, (RT, n), 1)
            return jnp.where(c <= r, s, -2.0 * BIG)

        s = masked(*tiles[0])
        for i, (h, half) in enumerate(tiles):
            nxt = masked(*tiles[i + 1]) if i < 7 else None
            mn, p = weights(s, None)
            rows = tile_rows(h, half)
            m_ref[rows] = mn
            acc_ref[rows] = jnp.dot(p, vals[:(half + 1) * RT], preferred_element_type=F32)
            s = nxt

    def put_mask(c, valid, n):
        kabuf[n * TOK:(n + 1) * TOK] = jnp.where(valid, 1.0 - onehot(c), 1.0).astype(BF)

    def two_blocks(ca, cb, part):
        keys = jnp.concatenate([
            jnp.concatenate([kvbuf[ca, 0], kvbuf[cb, 0]], axis=0), kabuf[...]], axis=1)
        vals = jnp.concatenate([
            jnp.concatenate([kvbuf[ca, 1], kvbuf[cb, 1]], axis=0), jnp.ones((2 * TOK, HW), BF)], axis=1)
        todo = tiles[part * 4:part * 4 + 4]
        s = scores(*todo[0], keys)
        for i, (h, half) in enumerate(todo):
            rows = tile_rows(h, half)
            mp = m_ref[rows]
            old = acc_ref[rows]
            nxt = scores(*todo[i + 1], keys) if i < 3 else None
            mn, p = weights(s, mp)
            al = jnp.exp2((mp - mn) * SCALE)
            add = jnp.dot(p, vals, preferred_element_type=F32)
            m_ref[rows] = mn
            acc_ref[rows] = old * jnp.concatenate([al, al], axis=1) + add
            s = nxt

    def kv_x1():
        for j, h in pieces:
            kv_wait(j, h, -1, 0, r1)
            if h == 0:
                kv_send(j, h, -1, 0, 1, 0, both(r1, x <= 2))
            kv_send(j, h, -1, 0, 0, 1, r1)
            kv_send(j, h, -1, 0, 0, -1, r1)

    def kv_back():
        outer = jnp.logical_or(x == 0, x == 3)
        for j in (0, 1):
            kv_wait(j, 1, 1, 0, outer)
            kv_send(j, 1, 1, 0, -1, 0, outer)

    def kv_row0():
        for j, h in pieces:
            kv_wait(j, h, 0, -1, z >= 1)
            kv_send(j, h, 0, -1, 0, 1, middle)

    def kv_x2():
        for j, h in pieces:
            kv_wait(j, h, -2, 0, r2)
            kv_send(j, h, -2, 0, 0, -1, both(r2, z >= 1))
            kv_send(j, h, -2, 0, 0, 1, both(r2, z == 3))

    def kv_row1():
        for j, h in pieces:
            kv_wait(j, h, -1, -1, r1)
            kv_send(j, h, -1, -1, 0, 1, both(r1, edge))
            kv_wait(j, h, -1, 1, r1)
            kv_send(j, h, -1, 1, 0, -1, both(r1, edge))

    def kv_row2():
        for j, h in pieces:
            kv_wait(j, h, -2, 1, both(r2, z <= 2))
            kv_send(j, h, -2, 1, 0, -1, both(r2, middle))

    def kv_last():
        for j, h in pieces:
            kv_wait(j, h, 0, -2, z >= 2)
            kv_wait(j, h, 0, 1, z == 3)
            kv_wait(j, h, -1, 2, r1)
            kv_wait(j, h, -2, -1, both(r2, z == 0))

    def kv_end():
        for j, h in pieces:
            kv_wait(j, h, -2, 2, both(r2, z <= 1))

    def w_own():
        for piece in (0, 1):
            for ddx in (-1, 1):
                w_send(0, piece, 0, ddx, w_hbm.at[pl.ds(piece * 512, 512)])

    def w_crossed():
        for piece in (0, 1):
            w_wait(1, piece, 0)
            for ddx in (-1, 1):
                w_send(1, piece, 0, ddx)

    def w_ring(s):
        for piece, a in ((0, -1), (1, 1)):
            w_wait(s, piece, a)
            w_send(s, piece, a, -a)
            w_wait(s, piece, -a)

    def w_far(s):
        for piece in (0, 1):
            w_wait(s, piece, 2)

    locals_[2].wait()
    pair[2].wait_recv()
    own_block()
    kv_x1()
    w_cross(1)
    kv_back()
    w_own()
    kv_row0()
    kv_x2()

    def pick(dz):
        zs = mod4(z + dz)
        before = zs < z
        c = jnp.where(before, x * 4, mod4(x - 2) * 4) + zs
        return c, jnp.logical_or(before, r2)

    steps = [
        ((chip_at(-1, 0), r1), (chip_at(-2, 0), r2)),
        ((chip_at(-1, -1), r1), (chip_at(-1, 1), r1)),
        ((chip_at(-1, 2), r1), pick(-1)),
        (pick(1), pick(2)),
    ]
    before = [[], [kv_row2], [kv_last], [kv_end]]
    between = [
        [[kv_row1], []],
        [[w_crossed], [lambda: w_ring(0)]],
        [[], [lambda: w_ring(1)]],
        [[], []],
    ]

    def a_slot(t, g, hh):
        return abuf.at[t, g, hh * RT:(hh + 1) * RT]

    def attended(hh):
        for h in range(4):
            rows = tile_rows(h, hh)
            abuf[0, core, hh * RT:(hh + 1) * RT, h * HW:(h + 1) * HW] = (
                acc_ref[rows, :HW] / acc_ref[rows, HW:]).astype(BF)
        send(a_slot(0, core, hh), a_slot(1, core, hh), a_recv.at[1, hh], (pair_chip * 2 + core, y))
        send(a_slot(0, core, hh), a_slot(0, core, hh), a_recv.at[0, hh], partner)

    for s in range(4):
        (ca, va), (cb, vb) = steps[s]
        for f in before[s]:
            f()
        live = jnp.logical_or(va, vb)
        ca = jnp.where(va, ca, chip)
        cb = jnp.where(vb, cb, chip)

        def masks():
            put_mask(ca, va, 0)
            put_mask(cb, vb, 1)

        pl.when(live)(masks)
        for part in (0, 1):
            pl.when(live)(lambda: two_blocks(ca, cb, part))
            for f in between[s][part]:
                f()
            if s == 3:
                attended(part)

    def project(t, hh):
        e = 2 * t + hh
        lhs = jnp.concatenate([abuf[t, 0, hh * RT:(hh + 1) * RT], abuf[t, 1, hh * RT:(hh + 1) * RT]], axis=1)

        def part(n):
            q = mod4(y + n)
            return jnp.dot(lhs, jnp.concatenate([wbuf[0, q], wbuf[1, q]], axis=1), preferred_element_type=F32)

        step = 1 if hh == 0 else -1
        far_out[e] = part(2).astype(BF)
        send(far_out.at[e], far_in.at[e], far_recv.at[e], y_at(step))
        back = 1 if step == -1 else 0
        near_out[e, 1 - back] = part(-step).astype(BF)
        send(near_out.at[e, 1 - back], near_in.at[e, 1 - back], near_recv.at[e, 1 - back], y_at(-step))
        hold[e] = part(step)
        own[e] = part(0)

    def forward(t, hh):
        e = 2 * t + hh
        step = 1 if hh == 0 else -1
        slot = 0 if step == 1 else 1
        wait(far_in.at[e], far_recv.at[e])
        near_out[e, slot] = (hold[e] + far_in[e].astype(F32)).astype(BF)
        send(near_out.at[e, slot], near_in.at[e, slot], near_recv.at[e, slot], y_at(step))

    out_cols = [pl.ds(pl.multiple_of((2 * zz + core) * HW, HW), HW) for zz in (z, 3 - z)]

    def finish(t, hh):
        e = 2 * t + hh
        for slot in (0, 1):
            wait(near_in.at[e, slot], near_recv.at[e, slot])
        fin[e] = (own[e] + near_in[e, 0].astype(F32) + near_in[e, 1].astype(F32)).astype(BF)
        for s in (0, 1):
            src = fin.at[e, :, pl.ds(s * HW, HW)]
            dst = out_hbm.at[:, out_cols[s]]
            if t == 1:
                send(src, dst, fin_recv.at[1 + core, s], (pair_chip * 2 + hh, y))
            else:
                pl.when(core == hh)(lambda: pltpu.make_async_copy(src, dst, fin_local.at[s]).start())
                send(src, dst, fin_recv.at[0, s], partner, core != hh)

    w_far(0)
    w_far(1)
    locals_[3].wait()
    for hh in (0, 1):
        wait(a_slot(0, 1 - core, hh), a_recv.at[0, hh])
        project(0, hh)

    def from_pair(hh):
        wait(a_slot(1, core, hh), a_recv.at[1, hh])
        send(a_slot(1, core, hh), a_slot(1, core, hh), a_recv.at[2, hh], partner)

    forward(0, 0)
    from_pair(0)
    forward(0, 1)
    wait(a_slot(1, 1 - core, 0), a_recv.at[2, 0])
    project(1, 0)
    finish(0, 0)
    from_pair(1)
    finish(0, 1)
    wait(a_slot(1, 1 - core, 1), a_recv.at[2, 1])
    project(1, 1)
    forward(1, 0)
    forward(1, 1)
    finish(1, 0)
    finish(1, 1)

    for s in (0, 1):
        for n in range(3):
            wait(out_hbm.at[:, out_cols[s]], fin_recv.at[n, s])
        pltpu.make_async_copy(fin.at[0, :, pl.ds(s * HW, HW)], out_hbm.at[:, out_cols[s]], fin_local.at[s]).wait()
    for c in pair:
        c.wait_send()
    for pred, make in sends:
        when(pred, lambda: make().wait_send())


def shards(queries, keys, values, segments, out_weight):
    anywhere = pl.BlockSpec(memory_space=pl.ANY)
    return pl.pallas_call(
        kernel,
        out_shape=jax.ShapeDtypeStruct((256, 1024), BF),
        in_specs=[anywhere, anywhere, anywhere, pl.BlockSpec(memory_space=pltpu.VMEM), anywhere],
        out_specs=anywhere,
        scratch_shapes=[
            pltpu.VMEM((TOK, 512), BF),
            pltpu.VMEM((16, 2, TOK, HW), BF),
            pltpu.VMEM((2 * TOK, HW), BF),
            pltpu.VMEM((2, 4, 1024, HW), BF),
            pltpu.VMEM((2048, HW), F32),
            pltpu.VMEM((2048, 2 * HW), F32),
            pltpu.VMEM((2, 2, TOK, 512), BF),
            pltpu.VMEM((4, RT, 256), F32),
            pltpu.VMEM((4, RT, 256), F32),
            pltpu.VMEM((4, RT, 256), BF),
            pltpu.VMEM((4, RT, 256), BF),
            pltpu.VMEM((4, 2, RT, 256), BF),
            pltpu.VMEM((4, 2, RT, 256), BF),
            pltpu.VMEM((4, RT, 256), BF),
            pltpu.SemaphoreType.DMA((4,)),
            pltpu.SemaphoreType.DMA((3,)),
            pltpu.SemaphoreType.DMA((3,)),
            pltpu.SemaphoreType.DMA((4, 16)),
            pltpu.SemaphoreType.DMA((4, 4)),
            pltpu.SemaphoreType.DMA((128,)),
            pltpu.SemaphoreType.DMA((3, 2)),
            pltpu.SemaphoreType.DMA((4,)),
            pltpu.SemaphoreType.DMA((4, 2)),
            pltpu.SemaphoreType.DMA((2,)),
            pltpu.SemaphoreType.DMA((3, 2)),
        ],
        compiler_params=pltpu.CompilerParams(
            collective_id=0, has_side_effects=True, vmem_limit_bytes=60 * 2**20),
        name="attention_projection",
    )(queries, keys, values, segments.reshape(64, HW), out_weight)


def solution(mesh):
    return jax.shard_map(
        shards,
        mesh=mesh,
        in_specs=(
            P("dense", "attn"),
            P("dense", "attn"),
            P("dense", "attn"),
            P(),
            P("attn", "dense"),
        ),
        out_specs=P("dense", "attn"),
        check_vma=False,
    )
```

```python
import math

import jax
import jax.numpy as jnp
from jax import lax
from jax.experimental import pallas as pl
from jax.experimental.pallas import tpu as pltpu
from jax.sharding import PartitionSpec as P

MESH = pl.DeviceIdType.MESH
BF = jnp.bfloat16
F32 = jnp.float32
HW = 128
TOK = 512
BIG = 32768.0
SCALE = math.log2(math.e) / math.sqrt(HW)
RT = 256
CHUNKS = ((0, 0, 256), (0, 256, 256), (1, 0, 128), (1, 128, 128), (1, 256, 128), (1, 384, 128))
N = len(CHUNKS)
STEPS = (
    ((-1, 0), (-1, -1)),
    ((-1, 1), (-2, 0)),
    ((-1, 2), (0, -1)),
    ((0, 1), (0, 2)),
)
ORDER = (
    ("ko", 0, 0), ("cr", 0), ("wo", 1, -1), ("ko", 1, 0), ("ko", 0, 1), ("ko", 1, 1), ("X1", 0, 0), ("X1", 0, 1),
    ("X1", 1, 0), ("X1", 1, 1), ("B", 1), ("B", 0), ("wo", 0, 1), ("X2", 0, 0), ("wo", 0, -1), ("wo", 1, 1),
    ("X2", 1, 0), ("X2", 1, 1), ("wr", 0, 1), ("cr", 1), ("wc", 0), ("L3", 0, 0), ("own",), ("Ra", 1, 0),
    ("X2", 0, 1), ("Ra", 0, 0), ("L1", 0, 1), ("Ra", 0, 1), ("R2", 1, 0), ("Rb", 0, 1), ("R0", 0, 0), ("Rb", 1, 0),
    ("R0", 0, 1), ("Rb", 1, 1), ("Rb", 0, 0), ("R2", 0, 0), ("wr", 0, 0), ("R2", 1, 1), ("c", 1, 0), ("c", 1, 1),
    ("R0", 1, 1), ("L3", 1, 1), ("wc", 1), ("R0", 1, 0), ("Ra", 1, 1), ("L3", 1, 0), ("c", 0, 0), ("R2", 0, 1),
    ("L0", 0, 1), ("c", 0, 1), ("L0", 1, 1), ("L0", 0, 0), ("E", 1, 0), ("E", 0, 0), ("L2", 1, 0), ("L1", 1, 0),
    ("L0", 1, 0), ("L2", 0, 1), ("wr", 1, 0), ("L1", 0, 0), ("ww", 0, 0), ("wr", 1, 1), ("E", 1, 1), ("L1", 1, 1),
    ("L2", 1, 1), ("L2", 0, 0), ("L3", 0, 1), ("wf", 0, 1), ("ww", 0, 1), ("c", 2, 0), ("E", 0, 1), ("c", 3, 0),
    ("at", 0), ("c", 2, 1), ("ww", 1, 1), ("ww", 1, 0), ("wf", 0, 0), ("h", 0), ("c", 3, 1), ("wf", 1, 1),
    ("wf", 1, 0), ("p", 0), ("at", 1), ("h", 1), ("p", 1), ("g", 2), ("g", 3), ("h", 2), ("p", 2), ("h", 3),
    ("g", 4), ("p", 3), ("f", 1), ("h", 4), ("p", 4), ("f", 2), ("g", 5), ("f", 4), ("h", 5), ("p", 5), ("f", 3),
    ("x", 2), ("x", 4), ("f", 0), ("f", 5), ("x", 3), ("x", 5), ("x", 1), ("x", 0),
)

def kernel(q_hbm, k_hbm, v_hbm, seg_ref, w_hbm, out_hbm,
           qbuf, kvbuf, kabuf, wbuf, m_ref, acc_ref, abuf, hold, own, far_out, far_in, near_out, near_in, fin,
           local_sem, pair_send, pair_recv, kv_recv, w_recv, send_sem, a_recv, far_recv, near_recv,
           fin_local, fin_recv):
    d = lax.axis_index("dense")
    y = lax.axis_index("attn")
    core = lax.rem(d, 2)
    chip = d // 2
    z = lax.rem(chip, 4)
    x = chip // 4

    def mod4(n):
        return lax.rem(n + 8, 4)

    def chip_at(dx, dz):
        return mod4(x + dx) * 4 + mod4(z + dz)

    def device_at(dx, dz):
        return (chip_at(dx, dz) * 2 + core, y)

    partner = (chip * 2 + (1 - core), y)
    pair_chip = x * 4 + (z + 1 - 2 * lax.rem(z, 2))
    cross = ((x * 4 + 3 - z) * 2 + core, y)

    def y_at(n):
        return (d, mod4(y + n))

    def when(pred, f):
        if pred is None:
            f()
        else:
            pl.when(pred)(f)

    def both(p, r):
        if p is None:
            return r
        if r is None:
            return p
        return jnp.logical_and(p, r)

    sends = []

    def send(src, dst, recv_sem, device, pred=None):
        n = len(sends)

        def make():
            return pltpu.make_async_remote_copy(
                src_ref=src, dst_ref=dst, send_sem=send_sem.at[n], recv_sem=recv_sem,
                device_id=device, device_id_type=MESH)

        sends.append((pred, make))
        when(pred, lambda: make().start())

    def wait(dst, recv_sem, pred=None):
        when(pred, lambda: pltpu.make_async_remote_copy(
            src_ref=dst, dst_ref=dst, send_sem=send_sem.at[0], recv_sem=recv_sem,
            device_id=partner, device_id_type=MESH).wait_recv())

    def kv_at(c, j, h):
        return kvbuf.at[c, j, pl.ds(pl.multiple_of(h * 256, 256), 256)]

    def kv_send(j, h, dx, dz, ddx, ddz, pred=None):
        slot = kv_at(chip_at(dx, dz), j, h)
        rel = ((dx - ddx) % 4) * 4 + (dz - ddz) % 4
        send(slot, slot, kv_recv.at[j * 2 + h, rel], device_at(ddx, ddz), pred)

    def kv_wait(j, h, dx, dz, pred=None):
        rel = (dx % 4) * 4 + dz % 4
        wait(kv_at(chip_at(dx, dz), j, h), kv_recv.at[j * 2 + h, rel], pred)

    pieces = [(j, h) for j in (0, 1) for h in (0, 1)]

    def w_at(s, row, piece):
        return wbuf.at[s, row, pl.ds(piece * 512, 512)]

    def w_send(s, piece, dx, ddx, src=None):
        slot = w_at(s, mod4(x + dx), piece)
        send(slot if src is None else src, slot, w_recv.at[s * 2 + piece, (dx - ddx) % 4], device_at(ddx, 0))

    def w_wait(s, piece, dx):
        wait(w_at(s, mod4(x + dx), piece), w_recv.at[s * 2 + piece, dx % 4])

    def cols_of(ref, width, which):
        return ref.at[:, pl.ds(pl.multiple_of(which * width, width), width)]

    rows_me = pl.ds(pl.multiple_of(core * 256, 256), 256)
    locals_ = [
        pltpu.make_async_copy(cols_of(k_hbm, HW, core), kv_at(chip, 0, core), local_sem.at[0]),
        pltpu.make_async_copy(cols_of(v_hbm, HW, core), kv_at(chip, 1, core), local_sem.at[1]),
        pltpu.make_async_copy(cols_of(q_hbm, 512, core), qbuf.at[rows_me], local_sem.at[2]),
        pltpu.make_async_copy(w_hbm, wbuf.at[0, x], local_sem.at[3]),
    ]
    for c in locals_:
        c.start()

    barrier = pltpu.get_barrier_semaphore()
    peers = [partner, device_at(1, 0), device_at(-1, 0), device_at(0, 1), device_at(0, -1),
             (pair_chip * 2 + (1 - core), y), y_at(1), y_at(-1)]
    for peer in peers:
        pl.semaphore_signal(barrier, inc=1, device_id=peer, device_id_type=MESH)
    pl.semaphore_wait(barrier, len(peers))

    pair = []
    for n, (src, dst) in enumerate((
            (cols_of(k_hbm, HW, 1 - core), kv_at(chip, 0, core)),
            (cols_of(v_hbm, HW, 1 - core), kv_at(chip, 1, core)),
            (cols_of(q_hbm, 512, 1 - core), qbuf.at[rows_me]))):
        pair.append(pltpu.make_async_remote_copy(
            src_ref=src, dst_ref=dst, send_sem=pair_send.at[n], recv_sem=pair_recv.at[n],
            device_id=partner, device_id_type=MESH))
        pair[-1].start()

    r1 = x >= 1
    r2 = x >= 2
    edge = jnp.logical_or(z == 0, z == 3)
    middle = jnp.logical_or(z == 1, z == 2)

    def kv_own(theirs, j):
        h = 1 - core if theirs else core
        if theirs:
            pair[j].wait_recv()
        else:
            locals_[j].wait()
        kv_send(j, h, 0, 0, 1, 0, x <= 2)
        kv_send(j, h, 0, 0, -1, 0, both(x <= 1, h == 1))
        kv_send(j, h, 0, 0, 0, 1, z <= 2)
        kv_send(j, h, 0, 0, 0, -1, z == 0)

    def w_cross(piece):
        send(w_hbm.at[pl.ds(piece * 512, 512)], w_at(1, x, piece), w_recv.at[2 + piece, 0], cross)

    def onehot(c):
        row = jnp.concatenate([seg_ref[pl.ds(c * 4 + i, 1), :] for i in range(4)], axis=1)
        hot = (lax.broadcasted_iota(jnp.int32, (HW, TOK), 0) == row).astype(F32)
        return hot.T

    own_hot = onehot(chip)
    qa = (own_hot * (-BIG)).astype(BF)

    def scores(h, half, keys):
        qq = qbuf[half * RT:(half + 1) * RT, h * HW:(h + 1) * HW]
        qc = jnp.concatenate([qq, qa[half * RT:(half + 1) * RT]], axis=1)
        return lax.dot_general(qc, keys, (((1,), (1,)), ((), ())), preferred_element_type=F32)

    def weights(s, mp):
        mc = jnp.max(s, axis=1, keepdims=True)
        mn = jnp.maximum(mp, mc) if mp is not None else jnp.broadcast_to(mc, (RT, HW))
        p = jnp.exp2(s * SCALE - (mn * SCALE)[:, :1])
        return mn, p.astype(BF)

    tiles = [(h, half) for half in range(2) for h in range(4)]

    def tile_rows(h, half):
        return slice((h * 2 + half) * RT, (h * 2 + half + 1) * RT)

    def own_block():
        keys = jnp.concatenate([kvbuf[chip, 0], (1.0 - own_hot).astype(BF)], axis=1)
        vals = jnp.concatenate([kvbuf[chip, 1], jnp.ones((TOK, HW), BF)], axis=1)

        def masked(h, half):
            n = (half + 1) * RT
            s = scores(h, half, keys[:n])
            r = lax.broadcasted_iota(jnp.int32, (RT, n), 0) + half * RT
            c = lax.broadcasted_iota(jnp.int32, (RT, n), 1)
            return jnp.where(c <= r, s, -2.0 * BIG)

        s = masked(*tiles[0])
        for i, (h, half) in enumerate(tiles):
            nxt = masked(*tiles[i + 1]) if i < 7 else None
            mn, p = weights(s, None)
            rows = tile_rows(h, half)
            m_ref[rows] = mn
            acc_ref[rows] = jnp.dot(p, vals[:(half + 1) * RT], preferred_element_type=F32)
            s = nxt

    def put_mask(si, c, valid, n):
        kabuf[si, n * TOK:(n + 1) * TOK] = jnp.where(valid, 1.0 - onehot(c), 1.0).astype(BF)

    def two_blocks(si, ca, cb, part):
        keys = jnp.concatenate([
            jnp.concatenate([kvbuf[ca, 0], kvbuf[cb, 0]], axis=0), kabuf[si]], axis=1)
        vals = jnp.concatenate([
            jnp.concatenate([kvbuf[ca, 1], kvbuf[cb, 1]], axis=0), jnp.ones((2 * TOK, HW), BF)], axis=1)
        todo = tiles[part * 4:part * 4 + 4]
        s = scores(*todo[0], keys)
        for i, (h, half) in enumerate(todo):
            rows = tile_rows(h, half)
            mp = m_ref[rows]
            old = acc_ref[rows]
            nxt = scores(*todo[i + 1], keys) if i < 3 else None
            mn, p = weights(s, mp)
            al = jnp.exp2((mp - mn) * SCALE)
            add = jnp.dot(p, vals, preferred_element_type=F32)
            m_ref[rows] = mn
            acc_ref[rows] = old * jnp.concatenate([al, al], axis=1) + add
            s = nxt

    outer = jnp.logical_or(x == 0, x == 3)

    def kv_x1(j, h):
        kv_wait(j, h, -1, 0, r1)
        if h == 0:
            kv_send(j, h, -1, 0, 1, 0, both(r1, x <= 2))
        kv_send(j, h, -1, 0, 0, 1, r1)
        kv_send(j, h, -1, 0, 0, -1, r1)

    def kv_back(j):
        kv_wait(j, 1, 1, 0, outer)
        kv_send(j, 1, 1, 0, -1, 0, outer)

    def kv_row0(j, h):
        kv_wait(j, h, 0, -1, z >= 1)
        kv_send(j, h, 0, -1, 0, 1, middle)

    def kv_x2(j, h):
        kv_wait(j, h, -2, 0, r2)
        kv_send(j, h, -2, 0, 0, -1, both(r2, z >= 1))
        kv_send(j, h, -2, 0, 0, 1, both(r2, z == 3))

    def kv_row1(a):
        def f(j, h):
            kv_wait(j, h, -1, a, r1)
            kv_send(j, h, -1, a, 0, -a, both(r1, edge))
        return f

    def kv_row2(j, h):
        kv_wait(j, h, -2, 1, both(r2, z <= 2))
        kv_send(j, h, -2, 1, 0, -1, both(r2, middle))

    def w_own(piece, ddx):
        w_send(0, piece, 0, ddx, w_hbm.at[pl.ds(piece * 512, 512)])

    def w_crossed(piece):
        w_wait(1, piece, 0)
        for ddx in (-1, 1):
            w_send(1, piece, 0, ddx)

    def w_ring(s, piece):
        a = 2 * piece - 1
        w_wait(s, piece, a)
        w_send(s, piece, a, -a)

    def pick(dz):
        zs = mod4(z + dz)
        before = zs < z
        c = jnp.where(before, x * 4, mod4(x - 2) * 4) + zs
        return c, jnp.logical_or(before, r2)

    def block(b):
        if b[0] == 0:
            return pick(b[1])
        return chip_at(*b), (r1 if b[0] == -1 else r2)

    def step(si, part):
        (ca, va), (cb, vb) = [block(b) for b in STEPS[si]]
        ca = jnp.where(va, ca, chip)
        cb = jnp.where(vb, cb, chip)

        def run():
            if part == 0:
                put_mask(si, ca, va, 0)
                put_mask(si, cb, vb, 1)
            two_blocks(si, ca, cb, part)

        pl.when(jnp.logical_or(va, vb))(run)

    def own_step():
        locals_[2].wait()
        pair[2].wait_recv()
        own_block()

    def a_slot(t, g, lo, n):
        return abuf.at[t, g, lo:lo + n]

    def attended(hh):
        for h in range(4):
            rows = tile_rows(h, hh)
            abuf[0, core, hh * RT:(hh + 1) * RT, h * HW:(h + 1) * HW] = (
                acc_ref[rows, :HW] / acc_ref[rows, HW:]).astype(BF)
        for e, (t, lo, n) in enumerate(CHUNKS):
            if lo // RT == hh:
                to = a_slot(t, core, lo, n)
                send(a_slot(0, core, lo, n), to, a_recv.at[e, 0],
                     (pair_chip * 2 + core, y) if t == 1 else partner)

    def way(e):
        return 1 if e % 2 == 0 else -1

    def near(e, up):
        n = CHUNKS[e][2]
        slot = 0 if up == 1 else 1
        return (near_out.at[e, slot, :n], near_in.at[e, slot, :n], near_recv.at[e, slot])

    def project(e):
        t, lo, n = CHUNKS[e]
        lhs = jnp.concatenate([abuf[t, 0, lo:lo + n], abuf[t, 1, lo:lo + n]], axis=1)

        def part(k):
            q = mod4(y + k)
            return jnp.dot(lhs, jnp.concatenate([wbuf[0, q], wbuf[1, q]], axis=1), preferred_element_type=F32)

        step = way(e)
        far_out[e, :n] = part(2).astype(BF)
        send(far_out.at[e, :n], far_in.at[e, :n], far_recv.at[e], y_at(step))
        src, dst, sem = near(e, -step)
        src[...] = part(-step).astype(BF)
        send(src, dst, sem, y_at(-step))
        hold[e, :n] = part(step)
        own[e, :n] = part(0)

    def forward(e):
        n = CHUNKS[e][2]
        step = way(e)
        wait(far_in.at[e, :n], far_recv.at[e])
        src, dst, sem = near(e, step)
        src[...] = (hold[e, :n] + far_in[e, :n].astype(F32)).astype(BF)
        send(src, dst, sem, y_at(step))

    out_cols = [pl.ds(pl.multiple_of((2 * zz + core) * HW, HW), HW) for zz in (z, 3 - z)]

    def finish(e):
        t, lo, n = CHUNKS[e]
        hh = lo // RT
        for up in (1, -1):
            _, dst, sem = near(e, up)
            wait(dst, sem)
        fin[e, :n] = (own[e, :n] + near_in[e, 0, :n].astype(F32) + near_in[e, 1, :n].astype(F32)).astype(BF)
        for s in (0, 1):
            src = fin.at[e, :n, pl.ds(s * HW, HW)]
            dst = out_hbm.at[pl.ds(lo - hh * RT, n), out_cols[s]]
            if t == 1:
                send(src, dst, fin_recv.at[e, core, s], (pair_chip * 2 + hh, y))
            else:
                pl.when(core == hh)(lambda: pltpu.make_async_copy(src, dst, fin_local.at[s]).start())
                send(src, dst, fin_recv.at[e, 0, s], partner, core != hh)

    def from_pair(e):
        _, lo, n = CHUNKS[e]
        wait(a_slot(1, core, lo, n), a_recv.at[e, 0])
        send(a_slot(1, core, lo, n), a_slot(1, core, lo, n), a_recv.at[e, 1], partner)

    def have(e):
        t, lo, n = CHUNKS[e]
        wait(a_slot(t, 1 - core, lo, n), a_recv.at[e, t])

    actions = {
        "ko": kv_own, "cr": w_cross, "own": own_step, "X1": kv_x1, "B": kv_back, "R0": kv_row0, "X2": kv_x2,
        "Ra": kv_row1(-1), "Rb": kv_row1(1), "R2": kv_row2,
        "L0": lambda j, h: kv_wait(j, h, 0, -2, z >= 2),
        "L1": lambda j, h: kv_wait(j, h, 0, 1, z == 3),
        "L2": lambda j, h: kv_wait(j, h, -1, 2, r1),
        "L3": lambda j, h: kv_wait(j, h, -2, -1, both(r2, z == 0)),
        "E": lambda j, h: kv_wait(j, h, -2, 2, both(r2, z <= 1)),
        "wo": w_own, "wc": w_crossed, "wr": w_ring,
        "ww": lambda s, piece: w_wait(s, piece, 1 - 2 * piece),
        "wf": lambda s, piece: w_wait(s, piece, 2),
        "c": step, "at": attended,
        "h": have, "p": project, "f": forward, "g": from_pair, "x": finish,
    }
    started = False
    for name, *args in ORDER:
        if name == "p" and not started:
            started = True
            locals_[3].wait()
        actions[name](*args)

    for s in (0, 1):
        for e, (t, lo, n) in enumerate(CHUNKS):
            hh = lo // RT
            dst = out_hbm.at[pl.ds(lo - hh * RT, n), out_cols[s]]
            if t == 1:
                for c in (0, 1):
                    wait(dst, fin_recv.at[e, c, s], core == hh)
            else:
                wait(dst, fin_recv.at[e, 0, s], core == hh)
        pltpu.make_async_copy(fin.at[0, :, pl.ds(s * HW, HW)], out_hbm.at[:, out_cols[s]], fin_local.at[s]).wait()
    for c in pair:
        c.wait_send()
    for pred, make in sends:
        when(pred, lambda: make().wait_send())


def shards(queries, keys, values, segments, out_weight):
    anywhere = pl.BlockSpec(memory_space=pl.ANY)
    return pl.pallas_call(
        kernel,
        out_shape=jax.ShapeDtypeStruct((256, 1024), BF),
        in_specs=[anywhere, anywhere, anywhere, pl.BlockSpec(memory_space=pltpu.VMEM), anywhere],
        out_specs=anywhere,
        scratch_shapes=[
            pltpu.VMEM((TOK, 512), BF),
            pltpu.VMEM((16, 2, TOK, HW), BF),
            pltpu.VMEM((4, 2 * TOK, HW), BF),
            pltpu.VMEM((2, 4, 1024, HW), BF),
            pltpu.VMEM((2048, HW), F32),
            pltpu.VMEM((2048, 2 * HW), F32),
            pltpu.VMEM((2, 2, TOK, 512), BF),
            pltpu.VMEM((N, RT, 256), F32),
            pltpu.VMEM((N, RT, 256), F32),
            pltpu.VMEM((N, RT, 256), BF),
            pltpu.VMEM((N, RT, 256), BF),
            pltpu.VMEM((N, 2, RT, 256), BF),
            pltpu.VMEM((N, 2, RT, 256), BF),
            pltpu.VMEM((N, RT, 256), BF),
            pltpu.SemaphoreType.DMA((4,)),
            pltpu.SemaphoreType.DMA((3,)),
            pltpu.SemaphoreType.DMA((3,)),
            pltpu.SemaphoreType.DMA((4, 16)),
            pltpu.SemaphoreType.DMA((4, 4)),
            pltpu.SemaphoreType.DMA((160,)),
            pltpu.SemaphoreType.DMA((N, 2)),
            pltpu.SemaphoreType.DMA((N,)),
            pltpu.SemaphoreType.DMA((N, 2)),
            pltpu.SemaphoreType.DMA((2,)),
            pltpu.SemaphoreType.DMA((N, 2, 2)),
        ],
        compiler_params=pltpu.CompilerParams(
            collective_id=0, has_side_effects=True, vmem_limit_bytes=60 * 2**20),
        name="attention_projection",
    )(queries, keys, values, segments.reshape(64, HW), out_weight)


def solution(mesh):
    return jax.shard_map(
        shards,
        mesh=mesh,
        in_specs=(
            P("dense", "attn"),
            P("dense", "attn"),
            P("dense", "attn"),
            P(),
            P("attn", "dense"),
        ),
        out_specs=P("dense", "attn"),
        check_vma=False,
    )
```

```python
import math

import jax
import jax.numpy as jnp
from jax import lax
from jax.experimental import pallas as pl
from jax.experimental.pallas import tpu as pltpu
from jax.sharding import PartitionSpec as P

MESH = pl.DeviceIdType.MESH
BF = jnp.bfloat16
F32 = jnp.float32
HW = 128
TOK = 512
BIG = 32768.0
SCALE = math.log2(math.e) / math.sqrt(HW)
RT = 256
CHUNKS = ((0, 0, 256, 2), (0, 256, 256, 2), (1, 0, 128, 2), (1, 128, 128, 2), (1, 256, 128, 2), (1, 384, 128, 2))
N = len(CHUNKS)
STEPS = (
    ((-1, 0),),
    ((-1, -1), (-1, 1)),
    ((-2, 0),),
    ((-1, 2),),
    ((0, -1),),
    ((0, 1),),
    ((0, 2),),
)
ORDER = (
    ("cr", 0), ("cr", 1), ("ko", 0, 0), ("ko", 0, 1), ("ko", 1, 1), ("ko", 1, 0), ("wo", 1, -1), ("X1", 0, 0),
    ("X1", 1, 0), ("wo", 0, 1), ("B", 0), ("B", 1), ("X1", 1, 1), ("wc", 0), ("own",), ("X2", 0, 0), ("X1", 0, 1),
    ("wc", 1), ("X2", 1, 1), ("wo", 0, -1), ("X2", 1, 0), ("X2", 0, 1), ("wr", 0, 0), ("c", 0, 0), ("L1", 1, 1),
    ("R2", 0, 0), ("wo", 1, 1), ("Ra", 0, 0), ("c", 2, 0), ("L1", 0, 1), ("R0", 0, 0), ("c", 0, 1), ("Ra", 1, 0),
    ("R2", 1, 1), ("R0", 1, 1), ("L1", 0, 0), ("wr", 0, 1), ("c", 2, 1), ("R2", 1, 0), ("Rb", 0, 0), ("R0", 0, 1),
    ("wr", 1, 0), ("ww", 1, 0), ("R0", 1, 0), ("wr", 1, 1), ("Ra", 1, 1), ("L1", 1, 0), ("L3", 1, 1), ("L3", 0, 0),
    ("L3", 1, 0), ("R2", 0, 1), ("c", 5, 0), ("L3", 0, 1), ("Ra", 0, 1), ("Rb", 1, 0), ("Rb", 1, 1), ("Rb", 0, 1),
    ("c", 1, 0), ("ww", 1, 1), ("c", 4, 0), ("L0", 0, 0), ("L2", 0, 0), ("c", 1, 1), ("E", 0, 0), ("E", 0, 1),
    ("L0", 1, 0), ("L0", 0, 1), ("E", 1, 0), ("E", 1, 1), ("L2", 1, 0), ("L0", 1, 1), ("c", 6, 0), ("L2", 1, 1),
    ("L2", 0, 1), ("c", 3, 0), ("at", 0), ("ww", 0, 1), ("c", 4, 1), ("c", 6, 1), ("wf", 0, 0), ("wf", 1, 0),
    ("wf", 0, 1), ("wf", 1, 1), ("h", 0), ("c", 5, 1), ("ww", 0, 0), ("p", 0), ("c", 3, 1), ("g", 2), ("at", 1),
    ("h", 2), ("p", 2), ("g", 3), ("h", 1), ("p", 1), ("h", 3), ("g", 4), ("p", 3), ("f", 2), ("h", 4), ("p", 4),
    ("g", 5), ("h", 5), ("p", 5), ("f", 3), ("x", 2), ("f", 4), ("f", 5), ("f", 1), ("f", 0), ("x", 3), ("x", 4),
    ("x", 5), ("x", 0), ("x", 1),
)

def kernel(q_hbm, k_hbm, v_hbm, seg_ref, w_hbm, out_hbm,
           qbuf, kvbuf, kabuf, wbuf, m_ref, acc_ref, abuf, hold, own, far_out, far_in, near_out, near_in, fin,
           local_sem, pair_send, pair_recv, kv_recv, w_recv, send_sem, a_recv, far_recv, near_recv,
           fin_local, fin_recv):
    d = lax.axis_index("dense")
    y = lax.axis_index("attn")
    core = lax.rem(d, 2)
    chip = d // 2
    z = lax.rem(chip, 4)
    x = chip // 4

    def mod4(n):
        return lax.rem(n + 8, 4)

    def chip_at(dx, dz):
        return mod4(x + dx) * 4 + mod4(z + dz)

    def device_at(dx, dz):
        return (chip_at(dx, dz) * 2 + core, y)

    partner = (chip * 2 + (1 - core), y)
    pair_chip = x * 4 + (z + 1 - 2 * lax.rem(z, 2))
    cross = ((x * 4 + 3 - z) * 2 + core, y)

    def y_at(n):
        return (d, mod4(y + n))

    def when(pred, f):
        if pred is None:
            f()
        else:
            pl.when(pred)(f)

    def both(p, r):
        if p is None:
            return r
        if r is None:
            return p
        return jnp.logical_and(p, r)

    sends = []

    def send(src, dst, recv_sem, device, pred=None):
        n = len(sends)

        def make():
            return pltpu.make_async_remote_copy(
                src_ref=src, dst_ref=dst, send_sem=send_sem.at[n], recv_sem=recv_sem,
                device_id=device, device_id_type=MESH)

        sends.append((pred, make))
        when(pred, lambda: make().start())

    def wait(dst, recv_sem, pred=None):
        when(pred, lambda: pltpu.make_async_remote_copy(
            src_ref=dst, dst_ref=dst, send_sem=send_sem.at[0], recv_sem=recv_sem,
            device_id=partner, device_id_type=MESH).wait_recv())

    def kv_at(c, j, h):
        return kvbuf.at[c, j, pl.ds(pl.multiple_of(h * 256, 256), 256)]

    def kv_send(j, h, dx, dz, ddx, ddz, pred=None):
        slot = kv_at(chip_at(dx, dz), j, h)
        rel = ((dx - ddx) % 4) * 4 + (dz - ddz) % 4
        send(slot, slot, kv_recv.at[j * 2 + h, rel], device_at(ddx, ddz), pred)

    def kv_wait(j, h, dx, dz, pred=None):
        rel = (dx % 4) * 4 + dz % 4
        wait(kv_at(chip_at(dx, dz), j, h), kv_recv.at[j * 2 + h, rel], pred)

    pieces = [(j, h) for j in (0, 1) for h in (0, 1)]

    def w_at(s, row, piece):
        return wbuf.at[s, row, pl.ds(piece * 512, 512)]

    def w_send(s, piece, dx, ddx, src=None):
        slot = w_at(s, mod4(x + dx), piece)
        send(slot if src is None else src, slot, w_recv.at[s * 2 + piece, (dx - ddx) % 4], device_at(ddx, 0))

    def w_wait(s, piece, dx):
        wait(w_at(s, mod4(x + dx), piece), w_recv.at[s * 2 + piece, dx % 4])

    def cols_of(ref, width, which):
        return ref.at[:, pl.ds(pl.multiple_of(which * width, width), width)]

    rows_me = pl.ds(pl.multiple_of(core * 256, 256), 256)
    locals_ = [
        pltpu.make_async_copy(cols_of(k_hbm, HW, core), kv_at(chip, 0, core), local_sem.at[0]),
        pltpu.make_async_copy(cols_of(v_hbm, HW, core), kv_at(chip, 1, core), local_sem.at[1]),
        pltpu.make_async_copy(cols_of(q_hbm, 512, core), qbuf.at[rows_me], local_sem.at[2]),
        pltpu.make_async_copy(w_hbm, wbuf.at[0, x], local_sem.at[3]),
    ]
    for c in locals_:
        c.start()

    barrier = pltpu.get_barrier_semaphore()
    peers = [partner, device_at(1, 0), device_at(-1, 0), device_at(0, 1), device_at(0, -1),
             (pair_chip * 2 + (1 - core), y), y_at(1), y_at(-1)]
    for peer in peers:
        pl.semaphore_signal(barrier, inc=1, device_id=peer, device_id_type=MESH)
    pl.semaphore_wait(barrier, len(peers))

    pair = []
    for n, (src, dst) in enumerate((
            (cols_of(k_hbm, HW, 1 - core), kv_at(chip, 0, core)),
            (cols_of(v_hbm, HW, 1 - core), kv_at(chip, 1, core)),
            (cols_of(q_hbm, 512, 1 - core), qbuf.at[rows_me]))):
        pair.append(pltpu.make_async_remote_copy(
            src_ref=src, dst_ref=dst, send_sem=pair_send.at[n], recv_sem=pair_recv.at[n],
            device_id=partner, device_id_type=MESH))
        pair[-1].start()

    r1 = x >= 1
    r2 = x >= 2
    edge = jnp.logical_or(z == 0, z == 3)
    middle = jnp.logical_or(z == 1, z == 2)

    def kv_own(theirs, j):
        h = 1 - core if theirs else core
        if theirs:
            pair[j].wait_recv()
        else:
            locals_[j].wait()
        kv_send(j, h, 0, 0, 1, 0, x <= 2)
        kv_send(j, h, 0, 0, -1, 0, both(x <= 1, h == 1))
        kv_send(j, h, 0, 0, 0, 1, z <= 2)
        kv_send(j, h, 0, 0, 0, -1, z == 0)

    def w_cross(piece):
        send(w_hbm.at[pl.ds(piece * 512, 512)], w_at(1, x, piece), w_recv.at[2 + piece, 0], cross)

    def onehot(c):
        row = jnp.concatenate([seg_ref[pl.ds(c * 4 + i, 1), :] for i in range(4)], axis=1)
        hot = (lax.broadcasted_iota(jnp.int32, (HW, TOK), 0) == row).astype(F32)
        return hot.T

    own_hot = onehot(chip)
    qa = (own_hot * (-BIG)).astype(BF)

    def scores(h, half, keys):
        qq = qbuf[half * RT:(half + 1) * RT, h * HW:(h + 1) * HW]
        qc = jnp.concatenate([qq, qa[half * RT:(half + 1) * RT]], axis=1)
        return lax.dot_general(qc, keys, (((1,), (1,)), ((), ())), preferred_element_type=F32)

    def weights(s, mp):
        mc = jnp.max(s, axis=1, keepdims=True)
        mn = jnp.maximum(mp, mc) if mp is not None else jnp.broadcast_to(mc, (RT, HW))
        p = jnp.exp2(s * SCALE - (mn * SCALE)[:, :1])
        return mn, p.astype(BF)

    tiles = [(h, half) for half in range(2) for h in range(4)]

    def tile_rows(h, half):
        return slice((h * 2 + half) * RT, (h * 2 + half + 1) * RT)

    def own_block():
        keys = jnp.concatenate([kvbuf[chip, 0], (1.0 - own_hot).astype(BF)], axis=1)
        vals = jnp.concatenate([kvbuf[chip, 1], jnp.ones((TOK, HW), BF)], axis=1)

        def masked(h, half):
            n = (half + 1) * RT
            s = scores(h, half, keys[:n])
            r = lax.broadcasted_iota(jnp.int32, (RT, n), 0) + half * RT
            c = lax.broadcasted_iota(jnp.int32, (RT, n), 1)
            return jnp.where(c <= r, s, -2.0 * BIG)

        s = masked(*tiles[0])
        for i, (h, half) in enumerate(tiles):
            nxt = masked(*tiles[i + 1]) if i < 7 else None
            mn, p = weights(s, None)
            rows = tile_rows(h, half)
            m_ref[rows] = mn
            acc_ref[rows] = jnp.dot(p, vals[:(half + 1) * RT], preferred_element_type=F32)
            s = nxt

    def put_mask(si, c, valid, n):
        kabuf[si, n * TOK:(n + 1) * TOK] = jnp.where(valid, 1.0 - onehot(c), 1.0).astype(BF)

    def more_blocks(si, part, far, *blocks):
        n = len(blocks) * TOK

        def rows_of(j):
            got = [kvbuf[c, j] for c in blocks]
            return got[0] if len(got) == 1 else jnp.concatenate(got, axis=0)

        keys = jnp.concatenate([rows_of(0), kabuf[si, :n]], axis=1)
        vals = jnp.concatenate([rows_of(1), jnp.ones((n, HW), BF)], axis=1)
        if far and part == 1:
            keys, vals = keys[RT:], vals[RT:]
        todo = tiles[part * 4:part * 4 + 4]
        s = scores(*todo[0], keys)
        for i, (h, half) in enumerate(todo):
            rows = tile_rows(h, half)
            mp = m_ref[rows]
            old = acc_ref[rows]
            nxt = scores(*todo[i + 1], keys) if i < 3 else None
            mn, p = weights(s, mp)
            al = jnp.exp2((mp - mn) * SCALE)
            add = jnp.dot(p, vals, preferred_element_type=F32)
            m_ref[rows] = mn
            acc_ref[rows] = old * jnp.concatenate([al, al], axis=1) + add
            s = nxt

    outer = jnp.logical_or(x == 0, x == 3)

    def kv_x1(j, h):
        kv_wait(j, h, -1, 0, r1)
        if h == 0:
            kv_send(j, h, -1, 0, 1, 0, both(r1, x <= 2))
        kv_send(j, h, -1, 0, 0, 1, r1)
        kv_send(j, h, -1, 0, 0, -1, r1)

    def kv_back(j):
        kv_wait(j, 1, 1, 0, outer)
        kv_send(j, 1, 1, 0, -1, 0, outer)

    def kv_row0(j, h):
        kv_wait(j, h, 0, -1, z >= 1)
        kv_send(j, h, 0, -1, 0, 1, middle)

    def kv_x2(j, h):
        kv_wait(j, h, -2, 0, r2)
        kv_send(j, h, -2, 0, 0, -1, both(r2, z >= 1))
        kv_send(j, h, -2, 0, 0, 1, both(r2, z == 3))

    def kv_row1(a):
        def f(j, h):
            kv_wait(j, h, -1, a, r1)
            kv_send(j, h, -1, a, 0, -a, both(r1, edge))
        return f

    def kv_row2(j, h):
        kv_wait(j, h, -2, 1, both(r2, z <= 2))
        kv_send(j, h, -2, 1, 0, -1, both(r2, middle))

    def w_own(piece, ddx):
        w_send(0, piece, 0, ddx, w_hbm.at[pl.ds(piece * 512, 512)])

    def w_crossed(piece):
        w_wait(1, piece, 0)
        for ddx in (-1, 1):
            w_send(1, piece, 0, ddx)

    def w_ring(s, piece):
        a = 2 * piece - 1
        w_wait(s, piece, a)
        w_send(s, piece, a, -a)

    def pick(dz):
        zs = mod4(z + dz)
        before = zs < z
        c = jnp.where(before, x * 4, mod4(x - 2) * 4) + zs
        return c, jnp.logical_or(before, r2)

    def block(b):
        if b[0] == 0:
            return pick(b[1])
        return chip_at(*b), (r1 if b[0] == -1 else r2)

    def step(si, part):
        got = [block(b) for b in STEPS[si]]
        live = got[0][1] if len(got) == 1 else jnp.logical_or(got[0][1], got[1][1])
        got = [(jnp.where(valid, c, chip), valid) for c, valid in got]

        def run():
            if part == 0:
                for n, (c, valid) in enumerate(got):
                    put_mask(si, c, valid, n)
            more_blocks(si, part, STEPS[si] == ((-2, 0),), *[c for c, valid in got])

        pl.when(live)(run)

    def own_step():
        locals_[2].wait()
        pair[2].wait_recv()
        own_block()

    def a_slot(t, g, lo, n):
        return abuf.at[t, g, lo:lo + n]

    def attended(hh):
        for h in range(4):
            rows = tile_rows(h, hh)
            abuf[0, core, hh * RT:(hh + 1) * RT, h * HW:(h + 1) * HW] = (
                acc_ref[rows, :HW] / acc_ref[rows, HW:]).astype(BF)
        for e, (t, lo, n, strips) in enumerate(CHUNKS):
            if lo // RT == hh and strips != 1:
                to = a_slot(t, core, lo, n)
                send(a_slot(0, core, lo, n), to, a_recv.at[e, 0],
                     (pair_chip * 2 + core, y) if t == 1 else partner)

    def way(e):
        return 1 if e % 2 == 0 else -1

    def part_of(e):
        t, lo, n, strips = CHUNKS[e]
        return pl.ds(0, n), pl.ds(0, 256 if strips == 2 else HW)

    def near(e, up):
        at = part_of(e)
        slot = 0 if up == 1 else 1
        return (near_out.at[(e, slot) + at], near_in.at[(e, slot) + at], near_recv.at[e, slot])

    def project(e):
        t, lo, n, strips = CHUNKS[e]
        at = (e,) + part_of(e)
        lhs = jnp.concatenate([abuf[t, 0, lo:lo + n], abuf[t, 1, lo:lo + n]], axis=1)

        def part(k):
            q = mod4(y + k)
            rhs = jnp.concatenate([wbuf[0, q], wbuf[1, q]], axis=1) if strips == 2 else wbuf[strips, q]
            return jnp.dot(lhs, rhs, preferred_element_type=F32)

        step = way(e)
        far_out[at] = part(2).astype(BF)
        send(far_out.at[at], far_in.at[at], far_recv.at[e], y_at(step))
        src, dst, sem = near(e, -step)
        src[...] = part(-step).astype(BF)
        send(src, dst, sem, y_at(-step))
        hold[at] = part(step)
        own[at] = part(0)

    def forward(e):
        at = (e,) + part_of(e)
        step = way(e)
        wait(far_in.at[at], far_recv.at[e])
        src, dst, sem = near(e, step)
        src[...] = (hold[at] + far_in[at].astype(F32)).astype(BF)
        send(src, dst, sem, y_at(step))

    out_cols = [pl.ds(pl.multiple_of((2 * zz + core) * HW, HW), HW) for zz in (z, 3 - z)]

    def strips_of(e):
        strips = CHUNKS[e][3]
        return ((0, 0), (1, HW)) if strips == 2 else ((strips, 0),)

    def finish(e):
        t, lo, n, strips = CHUNKS[e]
        hh = lo // RT
        at = (e,) + part_of(e)
        total = own[at]
        for up in (1, -1):
            _, dst, sem = near(e, up)
            wait(dst, sem)
            total += dst[...].astype(F32)
        fin[at] = total.astype(BF)
        for s, lane in strips_of(e):
            src = fin.at[e, :n, pl.ds(lane, HW)]
            dst = out_hbm.at[pl.ds(lo - hh * RT, n), out_cols[s]]
            if t == 1:
                send(src, dst, fin_recv.at[e, core, s], (pair_chip * 2 + hh, y))
            else:
                pl.when(core == hh)(lambda: pltpu.make_async_copy(src, dst, fin_local.at[e, s]).start())
                send(src, dst, fin_recv.at[e, 0, s], partner, core != hh)

    def from_pair(e):
        _, lo, n, strips = CHUNKS[e]
        wait(a_slot(1, core, lo, n), a_recv.at[e, 0])
        send(a_slot(1, core, lo, n), a_slot(1, core, lo, n), a_recv.at[e, 1], partner)

    def have(e):
        t, lo, n, strips = CHUNKS[e]
        wait(a_slot(t, 1 - core, lo, n), a_recv.at[e, t])

    actions = {
        "ko": kv_own, "cr": w_cross, "own": own_step, "X1": kv_x1, "B": kv_back, "R0": kv_row0, "X2": kv_x2,
        "Ra": kv_row1(-1), "Rb": kv_row1(1), "R2": kv_row2,
        "L0": lambda j, h: kv_wait(j, h, 0, -2, z >= 2),
        "L1": lambda j, h: kv_wait(j, h, 0, 1, z == 3),
        "L2": lambda j, h: kv_wait(j, h, -1, 2, r1),
        "L3": lambda j, h: kv_wait(j, h, -2, -1, both(r2, z == 0)),
        "E": lambda j, h: kv_wait(j, h, -2, 2, both(r2, z <= 1)),
        "wo": w_own, "wc": w_crossed, "wr": w_ring,
        "ww": lambda s, piece: w_wait(s, piece, 1 - 2 * piece),
        "wf": lambda s, piece: w_wait(s, piece, 2),
        "c": step, "at": attended,
        "h": have, "p": project, "f": forward, "g": from_pair, "x": finish,
    }
    started = False
    for name, *args in ORDER:
        if name == "p" and not started:
            started = True
            locals_[3].wait()
        actions[name](*args)

    for e, (t, lo, n, strips) in enumerate(CHUNKS):
        hh = lo // RT
        for s, lane in strips_of(e):
            dst = out_hbm.at[pl.ds(lo - hh * RT, n), out_cols[s]]
            if t == 1:
                for c in (0, 1):
                    wait(dst, fin_recv.at[e, c, s], core == hh)
            else:
                wait(dst, fin_recv.at[e, 0, s], core == hh)
                pl.when(core == hh)(lambda: pltpu.make_async_copy(
                    fin.at[e, :n, pl.ds(lane, HW)], dst, fin_local.at[e, s]).wait())
    for c in pair:
        c.wait_send()
    for pred, make in sends:
        when(pred, lambda: make().wait_send())


def shards(queries, keys, values, segments, out_weight):
    anywhere = pl.BlockSpec(memory_space=pl.ANY)
    return pl.pallas_call(
        kernel,
        out_shape=jax.ShapeDtypeStruct((256, 1024), BF),
        in_specs=[anywhere, anywhere, anywhere, pl.BlockSpec(memory_space=pltpu.VMEM), anywhere],
        out_specs=anywhere,
        scratch_shapes=[
            pltpu.VMEM((TOK, 512), BF),
            pltpu.VMEM((16, 2, TOK, HW), BF),
            pltpu.VMEM((len(STEPS), 2 * TOK, HW), BF),
            pltpu.VMEM((2, 4, 1024, HW), BF),
            pltpu.VMEM((2048, HW), F32),
            pltpu.VMEM((2048, 2 * HW), F32),
            pltpu.VMEM((2, 2, TOK, 512), BF),
            pltpu.VMEM((N, RT, 256), F32),
            pltpu.VMEM((N, RT, 256), F32),
            pltpu.VMEM((N, RT, 256), BF),
            pltpu.VMEM((N, RT, 256), BF),
            pltpu.VMEM((N, 2, RT, 256), BF),
            pltpu.VMEM((N, 2, RT, 256), BF),
            pltpu.VMEM((N, RT, 256), BF),
            pltpu.SemaphoreType.DMA((4,)),
            pltpu.SemaphoreType.DMA((3,)),
            pltpu.SemaphoreType.DMA((3,)),
            pltpu.SemaphoreType.DMA((4, 16)),
            pltpu.SemaphoreType.DMA((4, 4)),
            pltpu.SemaphoreType.DMA((192,)),
            pltpu.SemaphoreType.DMA((N, 2)),
            pltpu.SemaphoreType.DMA((N,)),
            pltpu.SemaphoreType.DMA((N, 2)),
            pltpu.SemaphoreType.DMA((N, 2)),
            pltpu.SemaphoreType.DMA((N, 2, 2)),
        ],
        compiler_params=pltpu.CompilerParams(
            collective_id=0, has_side_effects=True, vmem_limit_bytes=60 * 2**20),
        name="attention_projection",
    )(queries, keys, values, segments.reshape(64, HW), out_weight)


def solution(mesh):
    return jax.shard_map(
        shards,
        mesh=mesh,
        in_specs=(
            P("dense", "attn"),
            P("dense", "attn"),
            P("dense", "attn"),
            P(),
            P("attn", "dense"),
        ),
        out_specs=P("dense", "attn"),
        check_vma=False,
    )
```

```python
import math

import jax
import jax.numpy as jnp
from jax import lax
from jax.experimental import pallas as pl
from jax.experimental.pallas import tpu as pltpu
from jax.sharding import PartitionSpec as P

MESH = pl.DeviceIdType.MESH
BF = jnp.bfloat16
F32 = jnp.float32
HW = 128
TOK = 512
BIG = 32768.0
SCALE = math.log2(math.e) / math.sqrt(HW)
RT = 256
CHUNKS = ((0, 0, 256, 2), (0, 256, 256, 2), (1, 0, 128, 2), (1, 128, 128, 2), (1, 256, 128, 2), (1, 384, 128, 2))
N = len(CHUNKS)
STEPS = (
    ((-1, 0),),
    ((-2, 0),),
    ((-1, -1), (-1, 1)),
    ((-1, 2), (0, -1)),
    ((0, 1), (0, 2)),
)
ORDER = (
    ("cr", 0), ("cr", 1), ("ko", 0, 0), ("ko", 0, 1), ("ko", 1, 1), ("ko", 1, 0), ("own",), ("B", 1), ("X1", 0, 0),
    ("X1", 1, 0), ("wo", 0, 1), ("wc", 0), ("X2", 1, 1), ("B", 0), ("wo", 1, 1), ("wc", 1), ("X2", 0, 0),
    ("X1", 0, 1), ("ww", 1, 0), ("wo", 1, -1), ("X2", 1, 0), ("X2", 0, 1), ("X1", 1, 1), ("c", 0, 0), ("c", 0, 1),
    ("R2", 0, 0), ("c", 1, 0), ("R0", 0, 0), ("wr", 0, 0), ("R0", 0, 1), ("Ra", 1, 0), ("wr", 1, 0), ("wo", 0, -1),
    ("R2", 0, 1), ("R2", 1, 0), ("Ra", 0, 1), ("L1", 1, 1), ("wr", 1, 1), ("Rb", 0, 0), ("Ra", 0, 0), ("R0", 1, 0),
    ("c", 1, 1), ("Rb", 1, 0), ("L3", 0, 1), ("Ra", 1, 1), ("L3", 1, 1), ("Rb", 0, 1), ("Rb", 1, 1), ("R0", 1, 1),
    ("L1", 1, 0), ("wr", 0, 1), ("R2", 1, 1), ("L1", 0, 1), ("c", 2, 0), ("ww", 0, 1), ("L3", 0, 0), ("L1", 0, 0),
    ("c", 2, 1), ("L2", 1, 1), ("L2", 1, 0), ("L2", 0, 1), ("L3", 1, 0), ("E", 0, 1), ("E", 1, 1), ("L2", 0, 0),
    ("L0", 0, 0), ("c", 3, 0), ("E", 0, 0), ("E", 1, 0), ("ww", 1, 1), ("L0", 0, 1), ("L0", 1, 0), ("L0", 1, 1),
    ("c", 4, 0), ("at", 0), ("ww", 0, 0), ("c", 3, 1), ("wf", 0, 0), ("c", 4, 1), ("wf", 0, 1), ("h", 0),
    ("wf", 1, 1), ("wf", 1, 0), ("p", 0), ("g", 2), ("at", 1), ("h", 2), ("p", 2), ("g", 3), ("h", 1), ("p", 1),
    ("f", 2), ("g", 4), ("h", 3), ("p", 3), ("h", 4), ("p", 4), ("g", 5), ("h", 5), ("p", 5), ("f", 3), ("f", 4),
    ("x", 2), ("f", 0), ("f", 5), ("x", 3), ("f", 1), ("x", 4), ("x", 5), ("x", 0), ("x", 1),
)

def kernel(q_hbm, k_hbm, v_hbm, seg_ref, w_hbm, out_hbm,
           qbuf, kvbuf, kabuf, wbuf, m_ref, acc_ref, abuf, hold, own, far_out, far_in, near_out, near_in, fin,
           local_sem, pair_send, pair_recv, kv_recv, w_recv, send_sem, a_recv, far_recv, near_recv,
           fin_local, fin_recv):
    d = lax.axis_index("dense")
    y = lax.axis_index("attn")
    core = lax.rem(d, 2)
    chip = d // 2
    z = lax.rem(chip, 4)
    x = chip // 4

    def mod4(n):
        return lax.rem(n + 8, 4)

    def chip_at(dx, dz):
        return mod4(x + dx) * 4 + mod4(z + dz)

    def device_at(dx, dz):
        return (chip_at(dx, dz) * 2 + core, y)

    partner = (chip * 2 + (1 - core), y)
    pair_chip = x * 4 + (z + 1 - 2 * lax.rem(z, 2))
    cross = ((x * 4 + 3 - z) * 2 + core, y)

    def y_at(n):
        return (d, mod4(y + n))

    def when(pred, f):
        if pred is None:
            f()
        else:
            pl.when(pred)(f)

    def both(p, r):
        if p is None:
            return r
        if r is None:
            return p
        return jnp.logical_and(p, r)

    sends = []

    def send(src, dst, recv_sem, device, pred=None):
        n = len(sends)

        def make():
            return pltpu.make_async_remote_copy(
                src_ref=src, dst_ref=dst, send_sem=send_sem.at[n], recv_sem=recv_sem,
                device_id=device, device_id_type=MESH)

        sends.append((pred, make))
        when(pred, lambda: make().start())

    def wait(dst, recv_sem, pred=None):
        when(pred, lambda: pltpu.make_async_remote_copy(
            src_ref=dst, dst_ref=dst, send_sem=send_sem.at[0], recv_sem=recv_sem,
            device_id=partner, device_id_type=MESH).wait_recv())

    def kv_at(c, j, h):
        return kvbuf.at[c, j, pl.ds(pl.multiple_of(h * 256, 256), 256)]

    def kv_send(j, h, dx, dz, ddx, ddz, pred=None):
        slot = kv_at(chip_at(dx, dz), j, h)
        rel = ((dx - ddx) % 4) * 4 + (dz - ddz) % 4
        send(slot, slot, kv_recv.at[j * 2 + h, rel], device_at(ddx, ddz), pred)

    def kv_wait(j, h, dx, dz, pred=None):
        rel = (dx % 4) * 4 + dz % 4
        wait(kv_at(chip_at(dx, dz), j, h), kv_recv.at[j * 2 + h, rel], pred)

    pieces = [(j, h) for j in (0, 1) for h in (0, 1)]

    def w_at(s, row, piece):
        return wbuf.at[s, row, pl.ds(piece * 512, 512)]

    def w_send(s, piece, dx, ddx, src=None):
        slot = w_at(s, mod4(x + dx), piece)
        send(slot if src is None else src, slot, w_recv.at[s * 2 + piece, (dx - ddx) % 4], device_at(ddx, 0))

    def w_wait(s, piece, dx):
        wait(w_at(s, mod4(x + dx), piece), w_recv.at[s * 2 + piece, dx % 4])

    def cols_of(ref, width, which):
        return ref.at[:, pl.ds(pl.multiple_of(which * width, width), width)]

    rows_me = pl.ds(pl.multiple_of(core * 256, 256), 256)
    locals_ = [
        pltpu.make_async_copy(cols_of(k_hbm, HW, core), kv_at(chip, 0, core), local_sem.at[0]),
        pltpu.make_async_copy(cols_of(v_hbm, HW, core), kv_at(chip, 1, core), local_sem.at[1]),
        pltpu.make_async_copy(cols_of(q_hbm, 512, core), qbuf.at[rows_me], local_sem.at[2]),
        pltpu.make_async_copy(w_hbm, wbuf.at[0, x], local_sem.at[3]),
    ]
    for c in locals_:
        c.start()

    barrier = pltpu.get_barrier_semaphore()
    peers = [partner, device_at(1, 0), device_at(-1, 0), device_at(0, 1), device_at(0, -1),
             (pair_chip * 2 + (1 - core), y), y_at(1), y_at(-1)]
    for peer in peers:
        pl.semaphore_signal(barrier, inc=1, device_id=peer, device_id_type=MESH)
    pl.semaphore_wait(barrier, len(peers))

    pair = []
    for n, (src, dst) in enumerate((
            (cols_of(k_hbm, HW, 1 - core), kv_at(chip, 0, core)),
            (cols_of(v_hbm, HW, 1 - core), kv_at(chip, 1, core)),
            (cols_of(q_hbm, 512, 1 - core), qbuf.at[rows_me]))):
        pair.append(pltpu.make_async_remote_copy(
            src_ref=src, dst_ref=dst, send_sem=pair_send.at[n], recv_sem=pair_recv.at[n],
            device_id=partner, device_id_type=MESH))
        pair[-1].start()

    r1 = x >= 1
    r2 = x >= 2
    edge = jnp.logical_or(z == 0, z == 3)
    middle = jnp.logical_or(z == 1, z == 2)

    def kv_own(theirs, j):
        h = 1 - core if theirs else core
        if theirs:
            pair[j].wait_recv()
        else:
            locals_[j].wait()
        kv_send(j, h, 0, 0, 1, 0, x <= 2)
        kv_send(j, h, 0, 0, -1, 0, both(x <= 1, h == 1))
        kv_send(j, h, 0, 0, 0, 1, z <= 2)
        kv_send(j, h, 0, 0, 0, -1, z == 0)

    def w_cross(piece):
        send(w_hbm.at[pl.ds(piece * 512, 512)], w_at(1, x, piece), w_recv.at[2 + piece, 0], cross)

    def onehot(c):
        row = jnp.concatenate([seg_ref[pl.ds(c * 4 + i, 1), :] for i in range(4)], axis=1)
        hot = (lax.broadcasted_iota(jnp.int32, (HW, TOK), 0) == row).astype(F32)
        return hot.T

    own_hot = onehot(chip)
    qa = (own_hot * (-BIG)).astype(BF)

    def scores(h, half, keys):
        qq = qbuf[half * RT:(half + 1) * RT, h * HW:(h + 1) * HW]
        qc = jnp.concatenate([qq, qa[half * RT:(half + 1) * RT]], axis=1)
        return lax.dot_general(qc, keys, (((1,), (1,)), ((), ())), preferred_element_type=F32)

    def weights(s, mp):
        mc = jnp.max(s, axis=1, keepdims=True)
        mn = jnp.maximum(mp, mc) if mp is not None else jnp.broadcast_to(mc, (RT, HW))
        p = jnp.exp2(s * SCALE - (mn * SCALE)[:, :1])
        return mn, p.astype(BF)

    tiles = [(h, half) for half in range(2) for h in range(4)]

    def tile_rows(h, half):
        return slice((h * 2 + half) * RT, (h * 2 + half + 1) * RT)

    def own_block():
        keys = jnp.concatenate([kvbuf[chip, 0], (1.0 - own_hot).astype(BF)], axis=1)
        vals = jnp.concatenate([kvbuf[chip, 1], jnp.ones((TOK, HW), BF)], axis=1)

        def masked(h, half):
            n = (half + 1) * RT
            s = scores(h, half, keys[:n])
            r = lax.broadcasted_iota(jnp.int32, (RT, n), 0) + half * RT
            c = lax.broadcasted_iota(jnp.int32, (RT, n), 1)
            return jnp.where(c <= r, s, -2.0 * BIG)

        s = masked(*tiles[0])
        for i, (h, half) in enumerate(tiles):
            nxt = masked(*tiles[i + 1]) if i < 7 else None
            mn, p = weights(s, None)
            rows = tile_rows(h, half)
            m_ref[rows] = mn
            acc_ref[rows] = jnp.dot(p, vals[:(half + 1) * RT], preferred_element_type=F32)
            s = nxt

    def put_mask(si, c, valid, n):
        kabuf[si, n * TOK:(n + 1) * TOK] = jnp.where(valid, 1.0 - onehot(c), 1.0).astype(BF)

    def more_blocks(si, part, far, *blocks):
        n = len(blocks) * TOK

        def rows_of(j):
            got = [kvbuf[c, j] for c in blocks]
            return got[0] if len(got) == 1 else jnp.concatenate(got, axis=0)

        keys = jnp.concatenate([rows_of(0), kabuf[si, :n]], axis=1)
        vals = jnp.concatenate([rows_of(1), jnp.ones((n, HW), BF)], axis=1)
        if far and part == 1:
            keys, vals = keys[RT:], vals[RT:]
        todo = tiles[part * 4:part * 4 + 4]
        s = scores(*todo[0], keys)
        for i, (h, half) in enumerate(todo):
            rows = tile_rows(h, half)
            mp = m_ref[rows]
            old = acc_ref[rows]
            nxt = scores(*todo[i + 1], keys) if i < 3 else None
            mn, p = weights(s, mp)
            al = jnp.exp2((mp - mn) * SCALE)
            add = jnp.dot(p, vals, preferred_element_type=F32)
            m_ref[rows] = mn
            acc_ref[rows] = old * jnp.concatenate([al, al], axis=1) + add
            s = nxt

    outer = jnp.logical_or(x == 0, x == 3)

    def kv_x1(j, h):
        kv_wait(j, h, -1, 0, r1)
        if h == 0:
            kv_send(j, h, -1, 0, 1, 0, both(r1, x <= 2))
        kv_send(j, h, -1, 0, 0, 1, r1)
        kv_send(j, h, -1, 0, 0, -1, r1)

    def kv_back(j):
        kv_wait(j, 1, 1, 0, outer)
        kv_send(j, 1, 1, 0, -1, 0, outer)

    def kv_row0(j, h):
        kv_wait(j, h, 0, -1, z >= 1)
        kv_send(j, h, 0, -1, 0, 1, middle)

    def kv_x2(j, h):
        kv_wait(j, h, -2, 0, r2)
        kv_send(j, h, -2, 0, 0, -1, both(r2, z >= 1))
        kv_send(j, h, -2, 0, 0, 1, both(r2, z == 3))

    def kv_row1(a):
        def f(j, h):
            kv_wait(j, h, -1, a, r1)
            kv_send(j, h, -1, a, 0, -a, both(r1, edge))
        return f

    def kv_row2(j, h):
        kv_wait(j, h, -2, 1, both(r2, z <= 2))
        kv_send(j, h, -2, 1, 0, -1, both(r2, middle))

    def w_own(piece, ddx):
        w_send(0, piece, 0, ddx, w_hbm.at[pl.ds(piece * 512, 512)])

    def w_crossed(piece):
        w_wait(1, piece, 0)
        for ddx in (-1, 1):
            w_send(1, piece, 0, ddx)

    def w_ring(s, piece):
        a = 2 * piece - 1
        w_wait(s, piece, a)
        w_send(s, piece, a, -a)

    def pick(dz):
        zs = mod4(z + dz)
        before = zs < z
        c = jnp.where(before, x * 4, mod4(x - 2) * 4) + zs
        return c, jnp.logical_or(before, r2)

    def block(b):
        if b[0] == 0:
            return pick(b[1])
        return chip_at(*b), (r1 if b[0] == -1 else r2)

    def step(si, part):
        got = [block(b) for b in STEPS[si]]
        live = got[0][1] if len(got) == 1 else jnp.logical_or(got[0][1], got[1][1])
        got = [(jnp.where(valid, c, chip), valid) for c, valid in got]

        def run():
            if part == 0:
                for n, (c, valid) in enumerate(got):
                    put_mask(si, c, valid, n)
            more_blocks(si, part, STEPS[si] == ((-2, 0),), *[c for c, valid in got])

        pl.when(live)(run)

    def own_step():
        locals_[2].wait()
        pair[2].wait_recv()
        own_block()

    def a_slot(t, g, lo, n):
        return abuf.at[t, g, lo:lo + n]

    def attended(hh):
        for h in range(4):
            rows = tile_rows(h, hh)
            abuf[0, core, hh * RT:(hh + 1) * RT, h * HW:(h + 1) * HW] = (
                acc_ref[rows, :HW] / acc_ref[rows, HW:]).astype(BF)
        for e, (t, lo, n, strips) in enumerate(CHUNKS):
            if lo // RT == hh and strips != 1:
                to = a_slot(t, core, lo, n)
                send(a_slot(0, core, lo, n), to, a_recv.at[e, 0],
                     (pair_chip * 2 + core, y) if t == 1 else partner)

    def way(e):
        return 1 if e % 2 == 0 else -1

    def part_of(e):
        t, lo, n, strips = CHUNKS[e]
        return pl.ds(0, n), pl.ds(0, 256 if strips == 2 else HW)

    def near(e, up):
        at = part_of(e)
        slot = 0 if up == 1 else 1
        return (near_out.at[(e, slot) + at], near_in.at[(e, slot) + at], near_recv.at[e, slot])

    def project(e):
        t, lo, n, strips = CHUNKS[e]
        at = (e,) + part_of(e)
        lhs = jnp.concatenate([abuf[t, 0, lo:lo + n], abuf[t, 1, lo:lo + n]], axis=1)

        def part(k):
            q = mod4(y + k)
            rhs = jnp.concatenate([wbuf[0, q], wbuf[1, q]], axis=1) if strips == 2 else wbuf[strips, q]
            return jnp.dot(lhs, rhs, preferred_element_type=F32)

        step = way(e)
        far_out[at] = part(2).astype(BF)
        send(far_out.at[at], far_in.at[at], far_recv.at[e], y_at(step))
        src, dst, sem = near(e, -step)
        src[...] = part(-step).astype(BF)
        send(src, dst, sem, y_at(-step))
        hold[at] = part(step)
        own[at] = part(0)

    def forward(e):
        at = (e,) + part_of(e)
        step = way(e)
        wait(far_in.at[at], far_recv.at[e])
        src, dst, sem = near(e, step)
        src[...] = (hold[at] + far_in[at].astype(F32)).astype(BF)
        send(src, dst, sem, y_at(step))

    out_cols = [pl.ds(pl.multiple_of((2 * zz + core) * HW, HW), HW) for zz in (z, 3 - z)]

    def strips_of(e):
        strips = CHUNKS[e][3]
        return ((0, 0), (1, HW)) if strips == 2 else ((strips, 0),)

    def finish(e):
        t, lo, n, strips = CHUNKS[e]
        hh = lo // RT
        at = (e,) + part_of(e)
        total = own[at]
        for up in (1, -1):
            _, dst, sem = near(e, up)
            wait(dst, sem)
            total += dst[...].astype(F32)
        fin[at] = total.astype(BF)
        for s, lane in strips_of(e):
            src = fin.at[e, :n, pl.ds(lane, HW)]
            dst = out_hbm.at[pl.ds(lo - hh * RT, n), out_cols[s]]
            if t == 1:
                send(src, dst, fin_recv.at[e, core, s], (pair_chip * 2 + hh, y))
            else:
                pl.when(core == hh)(lambda: pltpu.make_async_copy(src, dst, fin_local.at[e, s]).start())
                send(src, dst, fin_recv.at[e, 0, s], partner, core != hh)

    def from_pair(e):
        _, lo, n, strips = CHUNKS[e]
        wait(a_slot(1, core, lo, n), a_recv.at[e, 0])
        send(a_slot(1, core, lo, n), a_slot(1, core, lo, n), a_recv.at[e, 1], partner)

    def have(e):
        t, lo, n, strips = CHUNKS[e]
        wait(a_slot(t, 1 - core, lo, n), a_recv.at[e, t])

    actions = {
        "ko": kv_own, "cr": w_cross, "own": own_step, "X1": kv_x1, "B": kv_back, "R0": kv_row0, "X2": kv_x2,
        "Ra": kv_row1(-1), "Rb": kv_row1(1), "R2": kv_row2,
        "L0": lambda j, h: kv_wait(j, h, 0, -2, z >= 2),
        "L1": lambda j, h: kv_wait(j, h, 0, 1, z == 3),
        "L2": lambda j, h: kv_wait(j, h, -1, 2, r1),
        "L3": lambda j, h: kv_wait(j, h, -2, -1, both(r2, z == 0)),
        "E": lambda j, h: kv_wait(j, h, -2, 2, both(r2, z <= 1)),
        "wo": w_own, "wc": w_crossed, "wr": w_ring,
        "ww": lambda s, piece: w_wait(s, piece, 1 - 2 * piece),
        "wf": lambda s, piece: w_wait(s, piece, 2),
        "c": step, "at": attended,
        "h": have, "p": project, "f": forward, "g": from_pair, "x": finish,
    }
    started = False
    for name, *args in ORDER:
        if name == "p" and not started:
            started = True
            locals_[3].wait()
        actions[name](*args)

    for e, (t, lo, n, strips) in enumerate(CHUNKS):
        hh = lo // RT
        for s, lane in strips_of(e):
            dst = out_hbm.at[pl.ds(lo - hh * RT, n), out_cols[s]]
            if t == 1:
                for c in (0, 1):
                    wait(dst, fin_recv.at[e, c, s], core == hh)
            else:
                wait(dst, fin_recv.at[e, 0, s], core == hh)
                pl.when(core == hh)(lambda: pltpu.make_async_copy(
                    fin.at[e, :n, pl.ds(lane, HW)], dst, fin_local.at[e, s]).wait())
    for c in pair:
        c.wait_send()
    for pred, make in sends:
        when(pred, lambda: make().wait_send())


def shards(queries, keys, values, segments, out_weight):
    anywhere = pl.BlockSpec(memory_space=pl.ANY)
    return pl.pallas_call(
        kernel,
        out_shape=jax.ShapeDtypeStruct((256, 1024), BF),
        in_specs=[anywhere, anywhere, anywhere, pl.BlockSpec(memory_space=pltpu.VMEM), anywhere],
        out_specs=anywhere,
        scratch_shapes=[
            pltpu.VMEM((TOK, 512), BF),
            pltpu.VMEM((16, 2, TOK, HW), BF),
            pltpu.VMEM((len(STEPS), 2 * TOK, HW), BF),
            pltpu.VMEM((2, 4, 1024, HW), BF),
            pltpu.VMEM((2048, HW), F32),
            pltpu.VMEM((2048, 2 * HW), F32),
            pltpu.VMEM((2, 2, TOK, 512), BF),
            pltpu.VMEM((N, RT, 256), F32),
            pltpu.VMEM((N, RT, 256), F32),
            pltpu.VMEM((N, RT, 256), BF),
            pltpu.VMEM((N, RT, 256), BF),
            pltpu.VMEM((N, 2, RT, 256), BF),
            pltpu.VMEM((N, 2, RT, 256), BF),
            pltpu.VMEM((N, RT, 256), BF),
            pltpu.SemaphoreType.DMA((4,)),
            pltpu.SemaphoreType.DMA((3,)),
            pltpu.SemaphoreType.DMA((3,)),
            pltpu.SemaphoreType.DMA((4, 16)),
            pltpu.SemaphoreType.DMA((4, 4)),
            pltpu.SemaphoreType.DMA((192,)),
            pltpu.SemaphoreType.DMA((N, 2)),
            pltpu.SemaphoreType.DMA((N,)),
            pltpu.SemaphoreType.DMA((N, 2)),
            pltpu.SemaphoreType.DMA((N, 2)),
            pltpu.SemaphoreType.DMA((N, 2, 2)),
        ],
        compiler_params=pltpu.CompilerParams(
            collective_id=0, has_side_effects=True, vmem_limit_bytes=60 * 2**20),
        name="attention_projection",
    )(queries, keys, values, segments.reshape(64, HW), out_weight)


def solution(mesh):
    return jax.shard_map(
        shards,
        mesh=mesh,
        in_specs=(
            P("dense", "attn"),
            P("dense", "attn"),
            P("dense", "attn"),
            P(),
            P("attn", "dense"),
        ),
        out_specs=P("dense", "attn"),
        check_vma=False,
    )
```

```python
import math

import jax
import jax.numpy as jnp
from jax import lax
from jax.experimental import pallas as pl
from jax.experimental.pallas import tpu as pltpu
from jax.sharding import PartitionSpec as P

MESH = pl.DeviceIdType.MESH
BF = jnp.bfloat16
F32 = jnp.float32
HW = 128
TOK = 512
BIG = 32768.0
SCALE = math.log2(math.e) / math.sqrt(HW)
RT = 256
CHUNKS = ((0, 0, 256, 2), (0, 256, 256, 2), (1, 0, 128, 2), (1, 128, 128, 2), (1, 256, 128, 2), (1, 384, 128, 2))
N = len(CHUNKS)
STEPS = (
    ((-1, 0),),
    ((-2, 0),),
    ((-1, -1), (-1, 1)),
    ((-1, 2), (0, -1)),
    ((0, 1), (0, 2)),
)
ORDER = (
    ("cr", 0), ("cr", 1), ("ko", 0, 0), ("ko", 0, 1), ("ko", 1, 1), ("ko", 1, 0), ("own",), ("B", 1), ("X1", 0, 0),
    ("X1", 1, 0), ("wo", 0, 1), ("wc", 0), ("X2", 1, 1), ("B", 0), ("wo", 1, 1), ("wc", 1), ("X2", 0, 0),
    ("X1", 0, 1), ("ww", 1, 0), ("wo", 1, -1), ("X2", 1, 0), ("X2", 0, 1), ("X1", 1, 1), ("c", 0, 0), ("c", 0, 1),
    ("R2", 0, 0), ("c", 1, 0), ("R0", 0, 0), ("wr", 0, 0), ("R0", 0, 1), ("Ra", 1, 0), ("wr", 1, 0), ("wo", 0, -1),
    ("R2", 0, 1), ("R2", 1, 0), ("Ra", 0, 1), ("L1", 1, 1), ("wr", 1, 1), ("Rb", 0, 0), ("Ra", 0, 0), ("R0", 1, 0),
    ("c", 1, 1), ("Rb", 1, 0), ("L3", 0, 1), ("Ra", 1, 1), ("L3", 1, 1), ("Rb", 0, 1), ("Rb", 1, 1), ("R0", 1, 1),
    ("L1", 1, 0), ("wr", 0, 1), ("R2", 1, 1), ("L1", 0, 1), ("c", 2, 0), ("ww", 0, 1), ("L3", 0, 0), ("L1", 0, 0),
    ("c", 2, 1), ("L2", 1, 1), ("L2", 1, 0), ("L2", 0, 1), ("L3", 1, 0), ("E", 0, 1), ("E", 1, 1), ("L2", 0, 0),
    ("L0", 0, 0), ("c", 3, 0), ("E", 0, 0), ("E", 1, 0), ("ww", 1, 1), ("L0", 0, 1), ("L0", 1, 0), ("L0", 1, 1),
    ("c", 4, 0), ("at", 0), ("ww", 0, 0), ("c", 3, 1), ("wf", 0, 0), ("c", 4, 1), ("wf", 0, 1), ("h", 0),
    ("wf", 1, 1), ("wf", 1, 0), ("p", 0), ("g", 2), ("at", 1), ("h", 2), ("p", 2), ("g", 3), ("h", 1), ("p", 1),
    ("f", 2), ("g", 4), ("h", 3), ("p", 3), ("h", 4), ("p", 4), ("g", 5), ("h", 5), ("p", 5), ("f", 3), ("f", 4),
    ("x", 2), ("f", 0), ("f", 5), ("x", 3), ("f", 1), ("x", 4), ("x", 5), ("x", 0), ("x", 1),
)

def kernel(q_hbm, k_hbm, v_hbm, seg_ref, w_hbm, out_hbm,
           qbuf, kvbuf, kabuf, wbuf, m_ref, acc_ref, abuf, hold, own, far_out, far_in, near_out, near_in, fin,
           local_sem, pair_send, pair_recv, kv_recv, w_recv, send_sem, a_recv, far_recv, near_recv,
           fin_local, fin_recv):
    d = lax.axis_index("dense")
    y = lax.axis_index("attn")
    core = lax.rem(d, 2)
    chip = d // 2
    z = lax.rem(chip, 4)
    x = chip // 4

    def mod4(n):
        return lax.rem(n + 8, 4)

    def chip_at(dx, dz):
        return mod4(x + dx) * 4 + mod4(z + dz)

    def device_at(dx, dz):
        return (chip_at(dx, dz) * 2 + core, y)

    partner = (chip * 2 + (1 - core), y)
    pair_chip = x * 4 + (z + 1 - 2 * lax.rem(z, 2))
    cross = ((x * 4 + 3 - z) * 2 + core, y)

    def y_at(n):
        return (d, mod4(y + n))

    def when(pred, f):
        if pred is None:
            f()
        else:
            pl.when(pred)(f)

    def both(p, r):
        if p is None:
            return r
        if r is None:
            return p
        return jnp.logical_and(p, r)

    sends = []

    def send(src, dst, recv_sem, device, pred=None):
        n = len(sends)

        def make():
            return pltpu.make_async_remote_copy(
                src_ref=src, dst_ref=dst, send_sem=send_sem.at[n], recv_sem=recv_sem,
                device_id=device, device_id_type=MESH)

        sends.append((pred, make))
        when(pred, lambda: make().start())

    def wait(dst, recv_sem, pred=None):
        when(pred, lambda: pltpu.make_async_remote_copy(
            src_ref=dst, dst_ref=dst, send_sem=send_sem.at[0], recv_sem=recv_sem,
            device_id=partner, device_id_type=MESH).wait_recv())

    def kv_at(c, j, h):
        return kvbuf.at[c, j, pl.ds(pl.multiple_of(h * 256, 256), 256)]

    def kv_send(j, h, dx, dz, ddx, ddz, pred=None):
        slot = kv_at(chip_at(dx, dz), j, h)
        rel = ((dx - ddx) % 4) * 4 + (dz - ddz) % 4
        send(slot, slot, kv_recv.at[j * 2 + h, rel], device_at(ddx, ddz), pred)

    def kv_wait(j, h, dx, dz, pred=None):
        rel = (dx % 4) * 4 + dz % 4
        wait(kv_at(chip_at(dx, dz), j, h), kv_recv.at[j * 2 + h, rel], pred)

    pieces = [(j, h) for j in (0, 1) for h in (0, 1)]

    def w_at(s, row, piece):
        return wbuf.at[s, row, pl.ds(piece * 512, 512)]

    def w_send(s, piece, dx, ddx, src=None):
        slot = w_at(s, mod4(x + dx), piece)
        send(slot if src is None else src, slot, w_recv.at[s * 2 + piece, (dx - ddx) % 4], device_at(ddx, 0))

    def w_wait(s, piece, dx):
        wait(w_at(s, mod4(x + dx), piece), w_recv.at[s * 2 + piece, dx % 4])

    def cols_of(ref, width, which):
        return ref.at[:, pl.ds(pl.multiple_of(which * width, width), width)]

    rows_me = pl.ds(pl.multiple_of(core * 256, 256), 256)
    locals_ = [
        pltpu.make_async_copy(cols_of(k_hbm, HW, core), kv_at(chip, 0, core), local_sem.at[0]),
        pltpu.make_async_copy(cols_of(v_hbm, HW, core), kv_at(chip, 1, core), local_sem.at[1]),
        pltpu.make_async_copy(cols_of(q_hbm, 512, core), qbuf.at[rows_me], local_sem.at[2]),
        pltpu.make_async_copy(w_hbm, wbuf.at[0, x], local_sem.at[3]),
    ]
    for c in locals_:
        c.start()

    barrier = pltpu.get_barrier_semaphore()
    peers = [partner, device_at(1, 0), device_at(-1, 0), device_at(0, 1), device_at(0, -1),
             (pair_chip * 2 + (1 - core), y), y_at(1), y_at(-1)]
    for peer in peers:
        pl.semaphore_signal(barrier, inc=1, device_id=peer, device_id_type=MESH)
    pl.semaphore_wait(barrier, len(peers))

    pair = []
    for n, (src, dst) in enumerate((
            (cols_of(k_hbm, HW, 1 - core), kv_at(chip, 0, core)),
            (cols_of(v_hbm, HW, 1 - core), kv_at(chip, 1, core)),
            (cols_of(q_hbm, 512, 1 - core), qbuf.at[rows_me]))):
        pair.append(pltpu.make_async_remote_copy(
            src_ref=src, dst_ref=dst, send_sem=pair_send.at[n], recv_sem=pair_recv.at[n],
            device_id=partner, device_id_type=MESH))
        pair[-1].start()

    r1 = x >= 1
    r2 = x >= 2
    edge = jnp.logical_or(z == 0, z == 3)
    middle = jnp.logical_or(z == 1, z == 2)

    def kv_own(theirs, j):
        h = 1 - core if theirs else core
        if theirs:
            pair[j].wait_recv()
        else:
            locals_[j].wait()
        kv_send(j, h, 0, 0, 1, 0, x <= 2)
        kv_send(j, h, 0, 0, -1, 0, both(x <= 1, h == 1))
        kv_send(j, h, 0, 0, 0, 1, z <= 2)
        kv_send(j, h, 0, 0, 0, -1, z == 0)

    def w_cross(piece):
        send(w_hbm.at[pl.ds(piece * 512, 512)], w_at(1, x, piece), w_recv.at[2 + piece, 0], cross)

    def onehot(c):
        row = jnp.concatenate([seg_ref[pl.ds(c * 4 + i, 1), :] for i in range(4)], axis=1)
        hot = (lax.broadcasted_iota(jnp.int32, (HW, TOK), 0) == row).astype(F32)
        return hot.T

    masks = {}

    def scores(h, half, keys):
        qq = qbuf[half * RT:(half + 1) * RT, h * HW:(h + 1) * HW]
        qc = jnp.concatenate([qq, masks["q"][half * RT:(half + 1) * RT]], axis=1)
        return lax.dot_general(qc, keys, (((1,), (1,)), ((), ())), preferred_element_type=F32)

    def weights(s, mp):
        mc = jnp.max(s, axis=1, keepdims=True)
        mn = jnp.maximum(mp, mc) if mp is not None else jnp.broadcast_to(mc, (RT, HW))
        p = jnp.exp2(s * SCALE - (mn * SCALE)[:, :1])
        return mn, p.astype(BF)

    tiles = [(h, half) for half in range(2) for h in range(4)]

    def tile_rows(h, half):
        return slice((h * 2 + half) * RT, (h * 2 + half + 1) * RT)

    def own_block():
        own_hot = onehot(chip)
        masks["q"] = (own_hot * (-BIG)).astype(BF)
        keys = jnp.concatenate([kvbuf[chip, 0], (1.0 - own_hot).astype(BF)], axis=1)
        vals = jnp.concatenate([kvbuf[chip, 1], jnp.ones((TOK, HW), BF)], axis=1)

        def masked(h, half):
            n = (half + 1) * RT
            s = scores(h, half, keys[:n])
            r = lax.broadcasted_iota(jnp.int32, (RT, n), 0) + half * RT
            c = lax.broadcasted_iota(jnp.int32, (RT, n), 1)
            return jnp.where(c <= r, s, -2.0 * BIG)

        s = masked(*tiles[0])
        for i, (h, half) in enumerate(tiles):
            nxt = masked(*tiles[i + 1]) if i < 7 else None
            mn, p = weights(s, None)
            rows = tile_rows(h, half)
            m_ref[rows] = mn
            acc_ref[rows] = jnp.dot(p, vals[:(half + 1) * RT], preferred_element_type=F32)
            s = nxt

    def put_mask(si, c, valid, n):
        kabuf[si, n * TOK:(n + 1) * TOK] = jnp.where(valid, 1.0 - onehot(c), 1.0).astype(BF)

    def more_blocks(si, part, far, *blocks):
        n = len(blocks) * TOK

        def rows_of(j):
            got = [kvbuf[c, j] for c in blocks]
            return got[0] if len(got) == 1 else jnp.concatenate(got, axis=0)

        keys = jnp.concatenate([rows_of(0), kabuf[si, :n]], axis=1)
        vals = jnp.concatenate([rows_of(1), jnp.ones((n, HW), BF)], axis=1)
        if far and part == 1:
            keys, vals = keys[RT:], vals[RT:]
        todo = tiles[part * 4:part * 4 + 4]
        s = scores(*todo[0], keys)
        for i, (h, half) in enumerate(todo):
            rows = tile_rows(h, half)
            mp = m_ref[rows]
            old = acc_ref[rows]
            nxt = scores(*todo[i + 1], keys) if i < 3 else None
            mn, p = weights(s, mp)
            al = jnp.exp2((mp - mn) * SCALE)
            add = jnp.dot(p, vals, preferred_element_type=F32)
            m_ref[rows] = mn
            acc_ref[rows] = old * jnp.concatenate([al, al], axis=1) + add
            s = nxt

    outer = jnp.logical_or(x == 0, x == 3)

    def kv_x1(j, h):
        kv_wait(j, h, -1, 0, r1)
        if h == 0:
            kv_send(j, h, -1, 0, 1, 0, both(r1, x <= 2))
        kv_send(j, h, -1, 0, 0, 1, r1)
        kv_send(j, h, -1, 0, 0, -1, r1)

    def kv_back(j):
        kv_wait(j, 1, 1, 0, outer)
        kv_send(j, 1, 1, 0, -1, 0, outer)

    def kv_row0(j, h):
        kv_wait(j, h, 0, -1, z >= 1)
        kv_send(j, h, 0, -1, 0, 1, middle)

    def kv_x2(j, h):
        kv_wait(j, h, -2, 0, r2)
        kv_send(j, h, -2, 0, 0, -1, both(r2, z >= 1))
        kv_send(j, h, -2, 0, 0, 1, both(r2, z == 3))

    def kv_row1(a):
        def f(j, h):
            kv_wait(j, h, -1, a, r1)
            kv_send(j, h, -1, a, 0, -a, both(r1, edge))
        return f

    def kv_row2(j, h):
        kv_wait(j, h, -2, 1, both(r2, z <= 2))
        kv_send(j, h, -2, 1, 0, -1, both(r2, middle))

    def w_own(piece, ddx):
        w_send(0, piece, 0, ddx, w_hbm.at[pl.ds(piece * 512, 512)])

    def w_crossed(piece):
        w_wait(1, piece, 0)
        for ddx in (-1, 1):
            w_send(1, piece, 0, ddx)

    def w_ring(s, piece):
        a = 2 * piece - 1
        w_wait(s, piece, a)
        w_send(s, piece, a, -a)

    def pick(dz):
        zs = mod4(z + dz)
        before = zs < z
        c = jnp.where(before, x * 4, mod4(x - 2) * 4) + zs
        return c, jnp.logical_or(before, r2)

    def block(b):
        if b[0] == 0:
            return pick(b[1])
        return chip_at(*b), (r1 if b[0] == -1 else r2)

    def step(si, part):
        got = [block(b) for b in STEPS[si]]
        live = got[0][1] if len(got) == 1 else jnp.logical_or(got[0][1], got[1][1])
        got = [(jnp.where(valid, c, chip), valid) for c, valid in got]

        def run():
            if part == 0:
                for n, (c, valid) in enumerate(got):
                    put_mask(si, c, valid, n)
            more_blocks(si, part, STEPS[si] == ((-2, 0),), *[c for c, valid in got])

        pl.when(live)(run)

    def own_step():
        locals_[2].wait()
        pair[2].wait_recv()
        own_block()

    def a_slot(t, g, lo, n):
        return abuf.at[t, g, lo:lo + n]

    def attended(hh):
        for h in range(4):
            rows = tile_rows(h, hh)
            abuf[0, core, hh * RT:(hh + 1) * RT, h * HW:(h + 1) * HW] = (
                acc_ref[rows, :HW] / acc_ref[rows, HW:]).astype(BF)
        for e, (t, lo, n, strips) in enumerate(CHUNKS):
            if lo // RT == hh and strips != 1:
                to = a_slot(t, core, lo, n)
                send(a_slot(0, core, lo, n), to, a_recv.at[e, 0],
                     (pair_chip * 2 + core, y) if t == 1 else partner)

    def way(e):
        return 1 if e % 2 == 0 else -1

    def part_of(e):
        t, lo, n, strips = CHUNKS[e]
        return pl.ds(0, n), pl.ds(0, 256 if strips == 2 else HW)

    def near(e, up):
        at = part_of(e)
        slot = 0 if up == 1 else 1
        return (near_out.at[(e, slot) + at], near_in.at[(e, slot) + at], near_recv.at[e, slot])

    def project(e):
        t, lo, n, strips = CHUNKS[e]
        at = (e,) + part_of(e)
        lhs = jnp.concatenate([abuf[t, 0, lo:lo + n], abuf[t, 1, lo:lo + n]], axis=1)

        def part(k):
            q = mod4(y + k)
            rhs = jnp.concatenate([wbuf[0, q], wbuf[1, q]], axis=1) if strips == 2 else wbuf[strips, q]
            return jnp.dot(lhs, rhs, preferred_element_type=F32)

        step = way(e)
        far_out[at] = part(2).astype(BF)
        send(far_out.at[at], far_in.at[at], far_recv.at[e], y_at(step))
        src, dst, sem = near(e, -step)
        src[...] = part(-step).astype(BF)
        send(src, dst, sem, y_at(-step))
        hold[at] = part(step)
        own[at] = part(0)

    def forward(e):
        at = (e,) + part_of(e)
        step = way(e)
        wait(far_in.at[at], far_recv.at[e])
        src, dst, sem = near(e, step)
        src[...] = (hold[at] + far_in[at].astype(F32)).astype(BF)
        send(src, dst, sem, y_at(step))

    out_cols = [pl.ds(pl.multiple_of((2 * zz + core) * HW, HW), HW) for zz in (z, 3 - z)]

    def strips_of(e):
        strips = CHUNKS[e][3]
        return ((0, 0), (1, HW)) if strips == 2 else ((strips, 0),)

    def finish(e):
        t, lo, n, strips = CHUNKS[e]
        hh = lo // RT
        at = (e,) + part_of(e)
        total = own[at]
        for up in (1, -1):
            _, dst, sem = near(e, up)
            wait(dst, sem)
            total += dst[...].astype(F32)
        fin[at] = total.astype(BF)
        for s, lane in strips_of(e):
            src = fin.at[e, :n, pl.ds(lane, HW)]
            dst = out_hbm.at[pl.ds(lo - hh * RT, n), out_cols[s]]
            if t == 1:
                send(src, dst, fin_recv.at[e, core, s], (pair_chip * 2 + hh, y))
            else:
                pl.when(core == hh)(lambda: pltpu.make_async_copy(src, dst, fin_local.at[e, s]).start())
                send(src, dst, fin_recv.at[e, 0, s], partner, core != hh)

    def from_pair(e):
        _, lo, n, strips = CHUNKS[e]
        wait(a_slot(1, core, lo, n), a_recv.at[e, 0])
        send(a_slot(1, core, lo, n), a_slot(1, core, lo, n), a_recv.at[e, 1], partner)

    def have(e):
        t, lo, n, strips = CHUNKS[e]
        wait(a_slot(t, 1 - core, lo, n), a_recv.at[e, t])

    actions = {
        "ko": kv_own, "cr": w_cross, "own": own_step, "X1": kv_x1, "B": kv_back, "R0": kv_row0, "X2": kv_x2,
        "Ra": kv_row1(-1), "Rb": kv_row1(1), "R2": kv_row2,
        "L0": lambda j, h: kv_wait(j, h, 0, -2, z >= 2),
        "L1": lambda j, h: kv_wait(j, h, 0, 1, z == 3),
        "L2": lambda j, h: kv_wait(j, h, -1, 2, r1),
        "L3": lambda j, h: kv_wait(j, h, -2, -1, both(r2, z == 0)),
        "E": lambda j, h: kv_wait(j, h, -2, 2, both(r2, z <= 1)),
        "wo": w_own, "wc": w_crossed, "wr": w_ring,
        "ww": lambda s, piece: w_wait(s, piece, 1 - 2 * piece),
        "wf": lambda s, piece: w_wait(s, piece, 2),
        "c": step, "at": attended,
        "h": have, "p": project, "f": forward, "g": from_pair, "x": finish,
    }
    started = False
    for name, *args in ORDER:
        if name == "p" and not started:
            started = True
            locals_[3].wait()
        actions[name](*args)

    for e, (t, lo, n, strips) in enumerate(CHUNKS):
        hh = lo // RT
        for s, lane in strips_of(e):
            dst = out_hbm.at[pl.ds(lo - hh * RT, n), out_cols[s]]
            if t == 1:
                for c in (0, 1):
                    wait(dst, fin_recv.at[e, c, s], core == hh)
            else:
                wait(dst, fin_recv.at[e, 0, s], core == hh)
                pl.when(core == hh)(lambda: pltpu.make_async_copy(
                    fin.at[e, :n, pl.ds(lane, HW)], dst, fin_local.at[e, s]).wait())
    for c in pair:
        c.wait_send()
    for pred, make in sends:
        when(pred, lambda: make().wait_send())


def shards(queries, keys, values, segments, out_weight):
    anywhere = pl.BlockSpec(memory_space=pl.ANY)
    return pl.pallas_call(
        kernel,
        out_shape=jax.ShapeDtypeStruct((256, 1024), BF),
        in_specs=[anywhere, anywhere, anywhere, pl.BlockSpec(memory_space=pltpu.VMEM), anywhere],
        out_specs=anywhere,
        scratch_shapes=[
            pltpu.VMEM((TOK, 512), BF),
            pltpu.VMEM((16, 2, TOK, HW), BF),
            pltpu.VMEM((len(STEPS), 2 * TOK, HW), BF),
            pltpu.VMEM((2, 4, 1024, HW), BF),
            pltpu.VMEM((2048, HW), F32),
            pltpu.VMEM((2048, 2 * HW), F32),
            pltpu.VMEM((2, 2, TOK, 512), BF),
            pltpu.VMEM((N, RT, 256), F32),
            pltpu.VMEM((N, RT, 256), F32),
            pltpu.VMEM((N, RT, 256), BF),
            pltpu.VMEM((N, RT, 256), BF),
            pltpu.VMEM((N, 2, RT, 256), BF),
            pltpu.VMEM((N, 2, RT, 256), BF),
            pltpu.VMEM((N, RT, 256), BF),
            pltpu.SemaphoreType.DMA((4,)),
            pltpu.SemaphoreType.DMA((3,)),
            pltpu.SemaphoreType.DMA((3,)),
            pltpu.SemaphoreType.DMA((4, 16)),
            pltpu.SemaphoreType.DMA((4, 4)),
            pltpu.SemaphoreType.DMA((192,)),
            pltpu.SemaphoreType.DMA((N, 2)),
            pltpu.SemaphoreType.DMA((N,)),
            pltpu.SemaphoreType.DMA((N, 2)),
            pltpu.SemaphoreType.DMA((N, 2)),
            pltpu.SemaphoreType.DMA((N, 2, 2)),
        ],
        compiler_params=pltpu.CompilerParams(
            collective_id=0, has_side_effects=True, vmem_limit_bytes=60 * 2**20),
        name="attention_projection",
    )(queries, keys, values, segments.reshape(64, HW), out_weight)


def solution(mesh):
    return jax.shard_map(
        shards,
        mesh=mesh,
        in_specs=(
            P("dense", "attn"),
            P("dense", "attn"),
            P("dense", "attn"),
            P(),
            P("attn", "dense"),
        ),
        out_specs=P("dense", "attn"),
        check_vma=False,
    )
```

```python
import math

import jax
import jax.numpy as jnp
from jax import lax
from jax.experimental import pallas as pl
from jax.experimental.pallas import tpu as pltpu
from jax.sharding import PartitionSpec as P

MESH = pl.DeviceIdType.MESH
BF = jnp.bfloat16
F32 = jnp.float32
HW = 128
TOK = 512
BIG = 32768.0
SCALE = math.log2(math.e) / math.sqrt(HW)
RT = 256
CHUNKS = ((0, 0, 256, 2), (0, 256, 256, 2), (1, 0, 128, 2), (1, 128, 128, 2), (1, 256, 128, 2), (1, 384, 128, 2))
N = len(CHUNKS)
STEPS = (
    ((-1, 0), (-2, 0)),
    ((-1, -1), (-1, 1)),
    ((-1, 2), (0, -1)),
    ((0, 1), (0, 2)),
)
ORDER = (
    ("cr", 0), ("cr", 1), ("ko", 0, 0), ("ko", 1, 0), ("ko", 0, 1), ("ko", 1, 1), ("wo", 1, -1), ("X1", 0, 0),
    ("B", 1), ("B", 0), ("X1", 1, 0), ("wc", 0), ("X1", 0, 1), ("X2", 0, 0), ("wo", 0, 1), ("X2", 1, 0), ("own",),
    ("X2", 0, 1), ("X1", 1, 1), ("wc", 1), ("X2", 1, 1), ("R0", 0, 0), ("R0", 1, 0), ("wr", 1, 0), ("Ra", 0, 0),
    ("wo", 0, -1), ("c", 0, 0), ("R2", 1, 0), ("wr", 0, 1), ("R0", 0, 1), ("R2", 0, 1), ("L1", 0, 1), ("L1", 0, 0),
    ("Ra", 0, 1), ("wo", 1, 1), ("Ra", 1, 0), ("Rb", 0, 0), ("c", 0, 1), ("R2", 1, 1), ("Ra", 1, 1), ("R2", 0, 0),
    ("R0", 1, 1), ("Rb", 0, 1), ("Rb", 1, 0), ("Rb", 1, 1), ("L3", 0, 0), ("wr", 0, 0), ("c", 1, 0), ("L3", 1, 1),
    ("wr", 1, 1), ("E", 0, 1), ("E", 1, 0), ("c", 1, 1), ("L0", 0, 1), ("L2", 0, 0), ("E", 0, 0), ("L3", 0, 1),
    ("L2", 0, 1), ("L2", 1, 1), ("L1", 1, 0), ("L3", 1, 0), ("L2", 1, 0), ("E", 1, 1), ("c", 2, 0), ("L1", 1, 1),
    ("L0", 0, 0), ("L0", 1, 1), ("L0", 1, 0), ("c", 3, 0), ("at", 0), ("c", 3, 1), ("ww", 1, 0), ("ww", 0, 0),
    ("ww", 0, 1), ("ww", 1, 1), ("h", 0), ("c", 2, 1), ("wf", 1, 1), ("wf", 0, 0), ("wf", 0, 1), ("wf", 1, 0),
    ("p", 0), ("g", 2), ("at", 1), ("h", 2), ("p", 2), ("h", 1), ("g", 3), ("p", 1), ("h", 3), ("g", 4), ("p", 3),
    ("f", 2), ("h", 4), ("p", 4), ("g", 5), ("h", 5), ("p", 5), ("f", 3), ("f", 4), ("x", 2), ("f", 5), ("f", 0),
    ("f", 1), ("x", 3), ("x", 4), ("x", 5), ("x", 0), ("x", 1),
)

def kernel(q_hbm, k_hbm, v_hbm, seg_ref, w_hbm, out_hbm,
           qbuf, kvbuf, kabuf, wbuf, m_ref, acc_ref, abuf, hold, own, far_out, far_in, near_out, near_in, fin,
           local_sem, pair_send, pair_recv, kv_recv, w_recv, send_sem, a_recv, far_recv, near_recv,
           fin_local, fin_recv):
    d = lax.axis_index("dense")
    y = lax.axis_index("attn")
    core = lax.rem(d, 2)
    chip = d // 2
    z = lax.rem(chip, 4)
    x = chip // 4

    def mod4(n):
        return lax.rem(n + 8, 4)

    def chip_at(dx, dz):
        return mod4(x + dx) * 4 + mod4(z + dz)

    def device_at(dx, dz):
        return (chip_at(dx, dz) * 2 + core, y)

    partner = (chip * 2 + (1 - core), y)
    pair_chip = x * 4 + (z + 1 - 2 * lax.rem(z, 2))
    cross = ((x * 4 + 3 - z) * 2 + core, y)

    def y_at(n):
        return (d, mod4(y + n))

    def when(pred, f):
        if pred is None:
            f()
        else:
            pl.when(pred)(f)

    def both(p, r):
        if p is None:
            return r
        if r is None:
            return p
        return jnp.logical_and(p, r)

    sends = []

    def send(src, dst, recv_sem, device, pred=None):
        n = len(sends)

        def make():
            return pltpu.make_async_remote_copy(
                src_ref=src, dst_ref=dst, send_sem=send_sem.at[n], recv_sem=recv_sem,
                device_id=device, device_id_type=MESH)

        sends.append((pred, make))
        when(pred, lambda: make().start())

    def wait(dst, recv_sem, pred=None):
        when(pred, lambda: pltpu.make_async_remote_copy(
            src_ref=dst, dst_ref=dst, send_sem=send_sem.at[0], recv_sem=recv_sem,
            device_id=partner, device_id_type=MESH).wait_recv())

    def kv_at(c, j, h):
        return kvbuf.at[c, j, pl.ds(pl.multiple_of(h * 256, 256), 256)]

    def kv_send(j, h, dx, dz, ddx, ddz, pred=None):
        slot = kv_at(chip_at(dx, dz), j, h)
        rel = ((dx - ddx) % 4) * 4 + (dz - ddz) % 4
        send(slot, slot, kv_recv.at[j * 2 + h, rel], device_at(ddx, ddz), pred)

    def kv_wait(j, h, dx, dz, pred=None):
        rel = (dx % 4) * 4 + dz % 4
        wait(kv_at(chip_at(dx, dz), j, h), kv_recv.at[j * 2 + h, rel], pred)

    pieces = [(j, h) for j in (0, 1) for h in (0, 1)]

    def w_at(s, row, piece):
        return wbuf.at[s, row, pl.ds(piece * 512, 512)]

    def w_send(s, piece, dx, ddx, src=None):
        slot = w_at(s, mod4(x + dx), piece)
        send(slot if src is None else src, slot, w_recv.at[s * 2 + piece, (dx - ddx) % 4], device_at(ddx, 0))

    def w_wait(s, piece, dx):
        wait(w_at(s, mod4(x + dx), piece), w_recv.at[s * 2 + piece, dx % 4])

    def cols_of(ref, width, which):
        return ref.at[:, pl.ds(pl.multiple_of(which * width, width), width)]

    rows_me = pl.ds(pl.multiple_of(core * 256, 256), 256)
    locals_ = [
        pltpu.make_async_copy(cols_of(k_hbm, HW, core), kv_at(chip, 0, core), local_sem.at[0]),
        pltpu.make_async_copy(cols_of(v_hbm, HW, core), kv_at(chip, 1, core), local_sem.at[1]),
        pltpu.make_async_copy(cols_of(q_hbm, 512, core), qbuf.at[rows_me], local_sem.at[2]),
        pltpu.make_async_copy(w_hbm, wbuf.at[0, x], local_sem.at[3]),
    ]
    for c in locals_:
        c.start()

    barrier = pltpu.get_barrier_semaphore()
    peers = [partner, device_at(1, 0), device_at(-1, 0), device_at(0, 1), device_at(0, -1),
             (pair_chip * 2 + (1 - core), y), y_at(1), y_at(-1)]
    for peer in peers:
        pl.semaphore_signal(barrier, inc=1, device_id=peer, device_id_type=MESH)
    pl.semaphore_wait(barrier, len(peers))

    pair = []
    for n, (src, dst) in enumerate((
            (cols_of(k_hbm, HW, 1 - core), kv_at(chip, 0, core)),
            (cols_of(v_hbm, HW, 1 - core), kv_at(chip, 1, core)),
            (cols_of(q_hbm, 512, 1 - core), qbuf.at[rows_me]))):
        pair.append(pltpu.make_async_remote_copy(
            src_ref=src, dst_ref=dst, send_sem=pair_send.at[n], recv_sem=pair_recv.at[n],
            device_id=partner, device_id_type=MESH))
        pair[-1].start()

    r1 = x >= 1
    r2 = x >= 2
    edge = jnp.logical_or(z == 0, z == 3)
    middle = jnp.logical_or(z == 1, z == 2)

    def kv_own(theirs, j):
        h = 1 - core if theirs else core
        if theirs:
            pair[j].wait_recv()
        else:
            locals_[j].wait()
        kv_send(j, h, 0, 0, 1, 0, x <= 2)
        kv_send(j, h, 0, 0, -1, 0, both(x <= 1, h == 1))
        kv_send(j, h, 0, 0, 0, 1, z <= 2)
        kv_send(j, h, 0, 0, 0, -1, z == 0)

    def w_cross(piece):
        send(w_hbm.at[pl.ds(piece * 512, 512)], w_at(1, x, piece), w_recv.at[2 + piece, 0], cross)

    def onehot(c):
        row = jnp.concatenate([seg_ref[pl.ds(c * 4 + i, 1), :] for i in range(4)], axis=1)
        hot = (lax.broadcasted_iota(jnp.int32, (HW, TOK), 0) == row).astype(F32)
        return hot.T

    masks = {}

    def scores(h, half, keys):
        qq = qbuf[half * RT:(half + 1) * RT, h * HW:(h + 1) * HW]
        qc = jnp.concatenate([qq, masks["q"][half * RT:(half + 1) * RT]], axis=1)
        return lax.dot_general(qc, keys, (((1,), (1,)), ((), ())), preferred_element_type=F32)

    def weights(s, mp):
        mc = jnp.max(s, axis=1, keepdims=True)
        mn = jnp.maximum(mp, mc) if mp is not None else jnp.broadcast_to(mc, (RT, HW))
        p = jnp.exp2(s * SCALE - (mn * SCALE)[:, :1])
        return mn, p.astype(BF)

    tiles = [(h, half) for half in range(2) for h in range(4)]

    def tile_rows(h, half):
        return slice((h * 2 + half) * RT, (h * 2 + half + 1) * RT)

    def own_block():
        own_hot = onehot(chip)
        masks["q"] = (own_hot * (-BIG)).astype(BF)
        keys = jnp.concatenate([kvbuf[chip, 0], (1.0 - own_hot).astype(BF)], axis=1)
        vals = jnp.concatenate([kvbuf[chip, 1], jnp.ones((TOK, HW), BF)], axis=1)

        def masked(h, half):
            n = (half + 1) * RT
            s = scores(h, half, keys[:n])
            r = lax.broadcasted_iota(jnp.int32, (RT, n), 0) + half * RT
            c = lax.broadcasted_iota(jnp.int32, (RT, n), 1)
            return jnp.where(c <= r, s, -2.0 * BIG)

        s = masked(*tiles[0])
        for i, (h, half) in enumerate(tiles):
            nxt = masked(*tiles[i + 1]) if i < 7 else None
            mn, p = weights(s, None)
            rows = tile_rows(h, half)
            m_ref[rows] = mn
            acc_ref[rows] = jnp.dot(p, vals[:(half + 1) * RT], preferred_element_type=F32)
            s = nxt

    def put_mask(si, c, valid, n):
        kabuf[si, n * TOK:(n + 1) * TOK] = jnp.where(valid, 1.0 - onehot(c), 1.0).astype(BF)

    def more_blocks(si, part, far, *blocks):
        n = len(blocks) * TOK

        def rows_of(j):
            got = [kvbuf[c, j] for c in blocks]
            return got[0] if len(got) == 1 else jnp.concatenate(got, axis=0)

        keys = jnp.concatenate([rows_of(0), kabuf[si, :n]], axis=1)
        vals = jnp.concatenate([rows_of(1), jnp.ones((n, HW), BF)], axis=1)
        if far and part == 1:
            keys, vals = keys[RT:], vals[RT:]
        todo = tiles[part * 4:part * 4 + 4]
        s = scores(*todo[0], keys)
        for i, (h, half) in enumerate(todo):
            rows = tile_rows(h, half)
            mp = m_ref[rows]
            old = acc_ref[rows]
            nxt = scores(*todo[i + 1], keys) if i < 3 else None
            mn, p = weights(s, mp)
            al = jnp.exp2((mp - mn) * SCALE)
            add = jnp.dot(p, vals, preferred_element_type=F32)
            m_ref[rows] = mn
            acc_ref[rows] = old * jnp.concatenate([al, al], axis=1) + add
            s = nxt

    outer = jnp.logical_or(x == 0, x == 3)

    def kv_x1(j, h):
        kv_wait(j, h, -1, 0, r1)
        if h == 0:
            kv_send(j, h, -1, 0, 1, 0, both(r1, x <= 2))
        kv_send(j, h, -1, 0, 0, 1, r1)
        kv_send(j, h, -1, 0, 0, -1, r1)

    def kv_back(j):
        kv_wait(j, 1, 1, 0, outer)
        kv_send(j, 1, 1, 0, -1, 0, outer)

    def kv_row0(j, h):
        kv_wait(j, h, 0, -1, z >= 1)
        kv_send(j, h, 0, -1, 0, 1, middle)

    def kv_x2(j, h):
        kv_wait(j, h, -2, 0, r2)
        kv_send(j, h, -2, 0, 0, -1, both(r2, z >= 1))
        kv_send(j, h, -2, 0, 0, 1, both(r2, z == 3))

    def kv_row1(a):
        def f(j, h):
            kv_wait(j, h, -1, a, r1)
            kv_send(j, h, -1, a, 0, -a, both(r1, edge))
        return f

    def kv_row2(j, h):
        kv_wait(j, h, -2, 1, both(r2, z <= 2))
        kv_send(j, h, -2, 1, 0, -1, both(r2, middle))

    def w_own(piece, ddx):
        w_send(0, piece, 0, ddx, w_hbm.at[pl.ds(piece * 512, 512)])

    def w_crossed(piece):
        w_wait(1, piece, 0)
        for ddx in (-1, 1):
            w_send(1, piece, 0, ddx)

    def w_ring(s, piece):
        a = 2 * piece - 1
        w_wait(s, piece, a)
        w_send(s, piece, a, -a)

    def pick(dz):
        zs = mod4(z + dz)
        before = zs < z
        c = jnp.where(before, x * 4, mod4(x - 2) * 4) + zs
        return c, jnp.logical_or(before, r2)

    def block(b):
        if b[0] == 0:
            return pick(b[1])
        return chip_at(*b), (r1 if b[0] == -1 else r2)

    def step(si, part):
        got = [block(b) for b in STEPS[si]]
        live = got[0][1] if len(got) == 1 else jnp.logical_or(got[0][1], got[1][1])
        got = [(jnp.where(valid, c, chip), valid) for c, valid in got]

        def run():
            if part == 0:
                for n, (c, valid) in enumerate(got):
                    put_mask(si, c, valid, n)
            more_blocks(si, part, STEPS[si] == ((-2, 0),), *[c for c, valid in got])

        pl.when(live)(run)

    def own_step():
        locals_[2].wait()
        pair[2].wait_recv()
        own_block()

    def a_slot(t, g, lo, n):
        return abuf.at[t, g, lo:lo + n]

    def attended(hh):
        for h in range(4):
            rows = tile_rows(h, hh)
            abuf[0, core, hh * RT:(hh + 1) * RT, h * HW:(h + 1) * HW] = (
                acc_ref[rows, :HW] / acc_ref[rows, HW:]).astype(BF)
        for e, (t, lo, n, strips) in enumerate(CHUNKS):
            if lo // RT == hh and strips != 1:
                to = a_slot(t, core, lo, n)
                send(a_slot(0, core, lo, n), to, a_recv.at[e, 0],
                     (pair_chip * 2 + core, y) if t == 1 else partner)

    def way(e):
        return 1 if e % 2 == 0 else -1

    def part_of(e):
        t, lo, n, strips = CHUNKS[e]
        return pl.ds(0, n), pl.ds(0, 256 if strips == 2 else HW)

    def near(e, up):
        at = part_of(e)
        slot = 0 if up == 1 else 1
        return (near_out.at[(e, slot) + at], near_in.at[(e, slot) + at], near_recv.at[e, slot])

    def project(e):
        t, lo, n, strips = CHUNKS[e]
        at = (e,) + part_of(e)
        lhs = jnp.concatenate([abuf[t, 0, lo:lo + n], abuf[t, 1, lo:lo + n]], axis=1)

        def part(k):
            q = mod4(y + k)
            rhs = jnp.concatenate([wbuf[0, q], wbuf[1, q]], axis=1) if strips == 2 else wbuf[strips, q]
            return jnp.dot(lhs, rhs, preferred_element_type=F32)

        step = way(e)
        far_out[at] = part(2).astype(BF)
        send(far_out.at[at], far_in.at[at], far_recv.at[e], y_at(step))
        src, dst, sem = near(e, -step)
        src[...] = part(-step).astype(BF)
        send(src, dst, sem, y_at(-step))
        hold[at] = part(step)
        own[at] = part(0)

    def forward(e):
        at = (e,) + part_of(e)
        step = way(e)
        wait(far_in.at[at], far_recv.at[e])
        src, dst, sem = near(e, step)
        src[...] = (hold[at] + far_in[at].astype(F32)).astype(BF)
        send(src, dst, sem, y_at(step))

    out_cols = [pl.ds(pl.multiple_of((2 * zz + core) * HW, HW), HW) for zz in (z, 3 - z)]

    def strips_of(e):
        strips = CHUNKS[e][3]
        return ((0, 0), (1, HW)) if strips == 2 else ((strips, 0),)

    def finish(e):
        t, lo, n, strips = CHUNKS[e]
        hh = lo // RT
        at = (e,) + part_of(e)
        total = own[at]
        for up in (1, -1):
            _, dst, sem = near(e, up)
            wait(dst, sem)
            total += dst[...].astype(F32)
        fin[at] = total.astype(BF)
        for s, lane in strips_of(e):
            src = fin.at[e, :n, pl.ds(lane, HW)]
            dst = out_hbm.at[pl.ds(lo - hh * RT, n), out_cols[s]]
            if t == 1:
                send(src, dst, fin_recv.at[e, core, s], (pair_chip * 2 + hh, y))
            else:
                pl.when(core == hh)(lambda: pltpu.make_async_copy(src, dst, fin_local.at[e, s]).start())
                send(src, dst, fin_recv.at[e, 0, s], partner, core != hh)

    def from_pair(e):
        _, lo, n, strips = CHUNKS[e]
        wait(a_slot(1, core, lo, n), a_recv.at[e, 0])
        send(a_slot(1, core, lo, n), a_slot(1, core, lo, n), a_recv.at[e, 1], partner)

    def have(e):
        t, lo, n, strips = CHUNKS[e]
        wait(a_slot(t, 1 - core, lo, n), a_recv.at[e, t])

    actions = {
        "ko": kv_own, "cr": w_cross, "own": own_step, "X1": kv_x1, "B": kv_back, "R0": kv_row0, "X2": kv_x2,
        "Ra": kv_row1(-1), "Rb": kv_row1(1), "R2": kv_row2,
        "L0": lambda j, h: kv_wait(j, h, 0, -2, z >= 2),
        "L1": lambda j, h: kv_wait(j, h, 0, 1, z == 3),
        "L2": lambda j, h: kv_wait(j, h, -1, 2, r1),
        "L3": lambda j, h: kv_wait(j, h, -2, -1, both(r2, z == 0)),
        "E": lambda j, h: kv_wait(j, h, -2, 2, both(r2, z <= 1)),
        "wo": w_own, "wc": w_crossed, "wr": w_ring,
        "ww": lambda s, piece: w_wait(s, piece, 1 - 2 * piece),
        "wf": lambda s, piece: w_wait(s, piece, 2),
        "c": step, "at": attended,
        "h": have, "p": project, "f": forward, "g": from_pair, "x": finish,
    }
    started = False
    for name, *args in ORDER:
        if name == "p" and not started:
            started = True
            locals_[3].wait()
        actions[name](*args)

    for e, (t, lo, n, strips) in enumerate(CHUNKS):
        hh = lo // RT
        for s, lane in strips_of(e):
            dst = out_hbm.at[pl.ds(lo - hh * RT, n), out_cols[s]]
            if t == 1:
                for c in (0, 1):
                    wait(dst, fin_recv.at[e, c, s], core == hh)
            else:
                wait(dst, fin_recv.at[e, 0, s], core == hh)
                pl.when(core == hh)(lambda: pltpu.make_async_copy(
                    fin.at[e, :n, pl.ds(lane, HW)], dst, fin_local.at[e, s]).wait())
    for c in pair:
        c.wait_send()
    for pred, make in sends:
        when(pred, lambda: make().wait_send())


def shards(queries, keys, values, segments, out_weight):
    anywhere = pl.BlockSpec(memory_space=pl.ANY)
    return pl.pallas_call(
        kernel,
        out_shape=jax.ShapeDtypeStruct((256, 1024), BF),
        in_specs=[anywhere, anywhere, anywhere, pl.BlockSpec(memory_space=pltpu.VMEM), anywhere],
        out_specs=anywhere,
        scratch_shapes=[
            pltpu.VMEM((TOK, 512), BF),
            pltpu.VMEM((16, 2, TOK, HW), BF),
            pltpu.VMEM((len(STEPS), 2 * TOK, HW), BF),
            pltpu.VMEM((2, 4, 1024, HW), BF),
            pltpu.VMEM((2048, HW), F32),
            pltpu.VMEM((2048, 2 * HW), F32),
            pltpu.VMEM((2, 2, TOK, 512), BF),
            pltpu.VMEM((N, RT, 256), F32),
            pltpu.VMEM((N, RT, 256), F32),
            pltpu.VMEM((N, RT, 256), BF),
            pltpu.VMEM((N, RT, 256), BF),
            pltpu.VMEM((N, 2, RT, 256), BF),
            pltpu.VMEM((N, 2, RT, 256), BF),
            pltpu.VMEM((N, RT, 256), BF),
            pltpu.SemaphoreType.DMA((4,)),
            pltpu.SemaphoreType.DMA((3,)),
            pltpu.SemaphoreType.DMA((3,)),
            pltpu.SemaphoreType.DMA((4, 16)),
            pltpu.SemaphoreType.DMA((4, 4)),
            pltpu.SemaphoreType.DMA((192,)),
            pltpu.SemaphoreType.DMA((N, 2)),
            pltpu.SemaphoreType.DMA((N,)),
            pltpu.SemaphoreType.DMA((N, 2)),
            pltpu.SemaphoreType.DMA((N, 2)),
            pltpu.SemaphoreType.DMA((N, 2, 2)),
        ],
        compiler_params=pltpu.CompilerParams(
            collective_id=0, has_side_effects=True, vmem_limit_bytes=60 * 2**20),
        name="attention_projection",
    )(queries, keys, values, segments.reshape(64, HW), out_weight)


def solution(mesh):
    return jax.shard_map(
        shards,
        mesh=mesh,
        in_specs=(
            P("dense", "attn"),
            P("dense", "attn"),
            P("dense", "attn"),
            P(),
            P("attn", "dense"),
        ),
        out_specs=P("dense", "attn"),
        check_vma=False,
    )
```
